512 devices in a mesh: wide: 64 (over x, z), narrow: 8 (over y, core).
Axes of the slice: x: 4, y: 4, z: 16, core: 2. Of those that a mesh axis runs over, the one named last changes fastest.
Arguments:
- frames: bfloat16 [16384, 1024], P('wide'), may hold values from -6 to 6
- expert_ids: int32 [16384, 2], P('wide'), may hold values from 0 to 63, all different within a row; in each aligned block of 256 rows (0 to 255, 256 to 511, ...) at most 16 rows name the same one
- gate_values: float32 [16384, 2], P('wide'), may hold values from 0.1 to 1
- w_gate: bfloat16 [64, 1024, 4096], P('wide', None, 'narrow'), may hold values from -0.1875 to 0.1875
- w_up: bfloat16 [64, 1024, 4096], P('wide', None, 'narrow'), may hold values from -0.1875 to 0.1875
- w_down: bfloat16 [64, 4096, 1024], P('wide', 'narrow'), may hold values from -0.09375 to 0.09375
- norm_gain: float32 [1024], replicated, may hold values from 0.1 to 1.9
- norm_bias: float32 [1024], replicated, may hold values from -2 to 2
- point_in: bfloat16 [1024, 2, 1024], P(None, None, 'narrow'), may hold values from -0.1875 to 0.1875
- depth_kernel: bfloat16 [31, 1024], P(None, 'narrow'), may hold values from -1 to 1
- point_out: bfloat16 [1024, 1024], P('narrow'), may hold values from -0.1875 to 0.1875
Outputs:
- block_out: bfloat16 [16384, 1024], P(('wide', 'narrow'))
The draws below stay inside these ranges and needn't reach their ends.
Inputs may be any that keep to these rules, and one draw needn't show every extreme that they name: `expert_ids`: each frame names 2 different experts; in each aligned block of 256 frames no expert is named by more than 16 frames, and every expert is named somewhere.
All inputs are finite; a program needn't handle non-finite values.
Results may differ from the reference program's by a relative error of at most 0.015.
Values may be sent and summed in bfloat16 or wider, within the bound.
No kernel may reach another device: no remote copies, remote signals or barrier semaphores. Data moves between devices by JAX's collectives and lax.ppermute only.
A program may use at most 64 MiB of HBM per device.

```python
import math
import jax
import jax.numpy as jnp
import numpy as np
from jax import lax

D = 1024
FF = 4096
TOP = 2
KERNEL = 31
TOK_GRP = 256
EXPERTS = 64
TOKENS = 16384
CAP = 16
N_WIDE = 64
N_NARROW = 8


def block_scale(key, dims, cuts, low, high):
    loudness = 1.0
    for dim, shards_of in cuts:
        draws = jax.random.uniform(jax.random.fold_in(jax.random.fold_in(key, 6), dim), (shards_of,), jnp.float32, low / len(cuts), high / len(cuts))
        loudness = loudness * jnp.repeat(jnp.exp(draws), dims[dim] // shards_of).reshape((-1,) + (1,) * (len(dims) - 1 - dim))
    return loudness


def routed_block(key, own, number, rows, count, top, reach, skew):
    sequence = jax.random.permutation(key, count)
    heavy_load, usual = portions_of(count, rows * top, reach, skew, True), portions_of(count, rows * top, reach, skew, False)
    places = jnp.arange(count)

    def named(tallies, turn):
        used = int((tallies > 0).sum())
        fixed = max(1, used // 4)
        moved = fixed + (places - fixed + turn * (used - fixed)) % max(1, count - fixed)
        return jnp.zeros((count,), jnp.int32).at[sequence[jnp.where(places < fixed, places, moved)]].set(jnp.asarray(tallies, jnp.int32))

    tallies = jnp.where(number % 4 == 0, named(heavy_load, number // 4), named(usual, number - number // 4 - 1))
    mixed = jax.random.permutation(jax.random.fold_in(own, 3), count)
    source_of, sink = mixed[0:count // 2 * 2:2], mixed[1:count // 2 * 2:2]
    slack = jnp.minimum(tallies[source_of] - 1, reach - tallies[sink]) // 2
    slack = jnp.where((source_of == sequence[0]) | (sink == sequence[0]) | (tallies[sink] == 0), 0, jnp.maximum(slack, 0))
    moved = jax.random.randint(jax.random.fold_in(own, 4), (count // 2,), 0, 1 << 20) % (slack + 1)
    tallies = tallies.at[source_of].add(-moved).at[sink].add(moved)
    items = jnp.searchsorted(jnp.cumsum(tallies), jnp.arange(rows * top), side="right").astype(jnp.int32)
    grid = items.reshape(top, rows).T
    grid = grid[jax.random.permutation(jax.random.fold_in(own, 1), rows)]
    turn = jax.random.randint(jax.random.fold_in(own, 2), (rows, 1), 0, top)
    return jnp.take_along_axis(grid, (jnp.arange(top)[None, :] + turn) % top, axis=1)


def portions_of(amount, total, bound, slope, full):
    weights = [(1 << 20) // math.isqrt(standing ** slope) + 1 for standing in range(1, amount + 1)]
    largest = bound if full else min(bound, max(-(-total // amount), total * weights[0] // sum(weights)))
    least = 1 if total - largest >= amount - 1 else 0
    holding, rest = [largest] + [least] * (amount - 1), total - largest - least * (amount - 1)
    while rest > 0:
        movable = [i for i in range(1, amount) if holding[i] < largest] or [i for i in range(1, amount) if holding[i] < bound]
        mass, left = sum([weights[i] for i in movable]), rest
        for i in movable:
            extra = min(bound - holding[i], max(1, left * weights[i] // mass), rest)
            holding[i] = holding[i] + extra
            rest = rest - extra
    return np.array(holding)


def centred(stream_key, dims, deviation, bound, shards=(), kind=jnp.bfloat16):
    result = deviation * jax.random.normal(stream_key, dims, jnp.float32)
    if shards:
        result = result * block_scale(stream_key, dims, shards, -0.22, 0.18)
    return jnp.clip(result, -bound, bound).astype(kind)


def setup_inputs(seed: int = 0) -> dict:
    key_of = jax.random.split(jax.random.key(seed), 12)
    frames = centred(key_of[0], (TOKENS, D), 1.0, 6.0, ((0, 64),))
    expert_ids_keys = jax.random.split(jax.random.fold_in(key_of[1], 1), TOKENS // TOK_GRP)
    expert_ids_turns = jax.random.permutation(jax.random.fold_in(key_of[1], 3), TOKENS // TOK_GRP)
    expert_ids = jax.vmap(lambda own, number: routed_block(jax.random.fold_in(key_of[1], 2), own, number, TOK_GRP, EXPERTS, TOP, CAP, 2))(expert_ids_keys, expert_ids_turns).reshape((TOKENS, TOP))
    gate_values = jnp.clip(0.1 + 0.9 * jax.random.uniform(key_of[2], (TOKENS, TOP), jnp.float32) ** block_scale(key_of[2], (TOKENS, TOP), ((0, 64),), -0.2, 0.2), 0.1, 1.0)
    w_gate = centred(key_of[3], (EXPERTS, D, FF), D ** -0.5, 0.1875, ((0, 64), (2, 8)))
    w_up = centred(key_of[4], (EXPERTS, D, FF), D ** -0.5, 0.1875, ((0, 64), (2, 8)))
    w_down = centred(key_of[5], (EXPERTS, FF, D), FF ** -0.5, 0.09375, ((0, 64), (1, 8)))
    norm_gain = jnp.clip(1.0 + 0.18 * jax.random.normal(key_of[6], (D,), jnp.float32), 0.1, 1.9)
    norm_bias = centred(key_of[7], (D,), 0.3, 2.0, (), jnp.float32)
    point_in = centred(key_of[8], (D, 2, D), D ** -0.5, 0.1875, ((2, 8),))
    depth_kernel = centred(key_of[9], (KERNEL, D), KERNEL ** -0.5, 1.0, ((1, 8),))
    point_out = centred(key_of[10], (D, D), D ** -0.5, 0.1875, ((0, 8),))
    return {"frames": frames, "expert_ids": expert_ids, "gate_values": gate_values, "w_gate": w_gate, "w_up": w_up, "w_down": w_down, "norm_gain": norm_gain, "norm_bias": norm_bias, "point_in": point_in, "depth_kernel": depth_kernel, "point_out": point_out}


def reference(frames, expert_ids, gate_values, w_gate, w_up, w_down, norm_gain, norm_bias, point_in, depth_kernel, point_out):
    total_rows = frames.shape[0]
    model_width = frames.shape[1]
    top_count = expert_ids.shape[1]
    grouped = expert_ids.reshape(N_WIDE, TOK_GRP * top_count)
    one_hot = (grouped[:, :, None] == jnp.arange(EXPERTS, dtype=jnp.int32)[None, None, :]).astype(jnp.int32)
    running = jnp.cumsum(one_hot, axis=1)
    slot_index = lax.optimization_barrier(jnp.sum((running - 1) * one_hot, axis=2))
    column = (jnp.arange(N_WIDE, dtype=jnp.int32)[:, None] * CAP + slot_index).reshape(-1).astype(jnp.int32)
    flat_ids = expert_ids.reshape(-1)
    token_index = (jnp.arange(total_rows * top_count, dtype=jnp.int32) // top_count).astype(jnp.int32)
    index_table = jnp.full((EXPERTS, N_WIDE * CAP), total_rows, jnp.int32).at[flat_ids, column].set(token_index)
    gate_table = jnp.zeros((EXPERTS, N_WIDE * CAP), jnp.float32).at[flat_ids, column].set(gate_values.reshape(-1).astype(jnp.float32))
    padded_frames = jnp.concatenate([frames, jnp.zeros((1, model_width), frames.dtype)], 0)
    block_size = FF // N_NARROW

    def one_expert(moe_sum, expert_index):
        picked = jnp.take(padded_frames, index_table[expert_index], axis=0)
        gate_all = w_gate[expert_index]
        up_all = w_up[expert_index]
        down_all = w_down[expert_index]
        output = jnp.zeros((N_WIDE * CAP, model_width), jnp.float32)
        for block_index in range(N_NARROW):
            low = block_index * block_size
            high = low + block_size
            gate_part = jnp.dot(picked, gate_all[:, low:high], preferred_element_type=jnp.float32)
            up_part = jnp.dot(picked, up_all[:, low:high], preferred_element_type=jnp.float32)
            hidden = (jax.nn.silu(gate_part) * up_part).astype(jnp.bfloat16)
            partial_value = jnp.dot(hidden, down_all[low:high, :], preferred_element_type=jnp.float32).astype(jnp.bfloat16)
            partial_value = lax.optimization_barrier(partial_value)
            output = output + partial_value.astype(jnp.float32)
        moe_sum = moe_sum.at[index_table[expert_index]].add(gate_table[expert_index][:, None] * output)
        return (moe_sum, None)
    moe_sum, _ = lax.scan(one_expert, jnp.zeros((total_rows + 1, model_width), jnp.float32), jnp.arange(EXPERTS, dtype=jnp.int32))
    residual = frames.astype(jnp.float32) + moe_sum[:total_rows]
    row_mean = lax.optimization_barrier(jnp.mean(residual, axis=1, keepdims=True))
    centered = residual - row_mean
    row_var = lax.optimization_barrier(jnp.mean(centered * centered, axis=1, keepdims=True))
    normed = (centered / jnp.sqrt(row_var + 1e-05) * norm_gain[None, :] + norm_bias[None, :]).astype(jnp.bfloat16)
    value_half = jnp.dot(normed, point_in[:, 0, :], preferred_element_type=jnp.float32)
    gate_half = jnp.dot(normed, point_in[:, 1, :], preferred_element_type=jnp.float32)
    glu_out = (value_half * jax.nn.sigmoid(gate_half)).astype(jnp.bfloat16)
    half_width = (KERNEL - 1) // 2
    padded = jnp.pad(glu_out, ((half_width, half_width), (0, 0)))
    depthwise = jnp.zeros((total_rows, model_width), jnp.float32)
    for tap_index in range(KERNEL):
        depthwise = depthwise + padded[tap_index:tap_index + total_rows].astype(jnp.float32) * depth_kernel[tap_index].astype(jnp.float32)[None, :]
    activated = (depthwise * jax.nn.sigmoid(depthwise)).astype(jnp.bfloat16)
    return (residual + jnp.dot(activated, point_out, preferred_element_type=jnp.float32)).astype(jnp.bfloat16)
```

```python
import jax
import jax.numpy as jnp
from jax import lax
from jax.experimental import pallas as pl
from jax.experimental.pallas import tpu as pltpu
from jax.sharding import Mesh
from jax.sharding import PartitionSpec as P

WIDE = ("x", "z")
NARROW = ("y", "c")
EVERY = ("x", "z", "y", "c")
VMEM_BYTES = 48 << 20


def in_vmem(count):
    return [pl.BlockSpec(memory_space=pltpu.VMEM)] * count


def mm(a, b):
    return jnp.dot(a, b, preferred_element_type=jnp.float32)


def route_kernel(experts, slots, pos_ref, ids_ref, frames_ref, out_ref, target_ref):
    count = ids_ref.shape[1]
    first = pos_ref[1] * slots
    expert = lax.broadcasted_iota(jnp.int32, (experts, count), 0)
    named = [jnp.where(expert == ids_ref[k : k + 1, :], 1.0, 0.0) for k in range(2)]
    before = lax.broadcasted_iota(jnp.int32, (count, count), 0) < lax.broadcasted_iota(
        jnp.int32, (count, count), 1
    )
    rank = mm(
        jnp.concatenate(named, axis=0).astype(jnp.bfloat16),
        jnp.where(before, 1.0, 0.0).astype(jnp.bfloat16),
    )
    held = jnp.sum(named[0], axis=1, keepdims=True)
    place = [
        jnp.sum(named[0] * rank[:experts], axis=0, keepdims=True),
        jnp.sum(named[1] * (rank[experts:] + held), axis=0, keepdims=True),
    ]
    row = lax.broadcasted_iota(jnp.int32, (experts * slots, count), 0)
    chosen = None
    for k in range(2):
        local = place[k].astype(jnp.int32) - first
        target = jnp.where(
            (local >= 0) & (local < slots), ids_ref[k : k + 1, :] * slots + local, -1
        )
        target_ref[k : k + 1, :] = target.astype(jnp.float32)
        hit = row == target
        chosen = hit if chosen is None else chosen | hit
    out_ref[...] = mm(
        jnp.where(chosen, 1.0, 0.0).astype(jnp.bfloat16), frames_ref[...]
    ).astype(jnp.bfloat16)


def expert_kernel(x_ref, *refs):
    out_ref = refs[-1]
    chunks, _, width = x_ref.shape
    total = None
    for pair in range(2):
        gate_ref, up_ref, down_ref = refs[3 * pair : 3 * pair + 3]
        gate = up = None
        for q in range(chunks):
            rows = slice(q * width, (q + 1) * width)
            g, u = mm(x_ref[q], gate_ref[rows, :]), mm(x_ref[q], up_ref[rows, :])
            gate, up = (g, u) if gate is None else (gate + g, up + u)
        hidden = (gate * jax.nn.sigmoid(gate) * up).astype(jnp.bfloat16)
        part = mm(hidden, down_ref[...])
        total = part if total is None else total + part
    for q in range(chunks):
        out_ref[q] = total[:, q * width : (q + 1) * width].astype(jnp.bfloat16)


def combine_kernel(target_ref, gate_ref, rows_ref, out_ref):
    count = target_ref.shape[1]
    table = jnp.concatenate(
        [target_ref[...], gate_ref[...], jnp.zeros((4, count), jnp.float32)], axis=0
    ).T
    slot = lax.broadcasted_iota(jnp.int32, (count, rows_ref.shape[0]), 1)
    total = None
    for k in range(2):
        hit = slot == table[:, k : k + 1].astype(jnp.int32)
        picked = mm(jnp.where(hit, 1.0, 0.0).astype(jnp.bfloat16), rows_ref[...])
        picked = picked * table[:, 2 + k : 3 + k]
        total = picked if total is None else total + picked
    out_ref[...] = total.astype(jnp.bfloat16)


def norm_kernel(pos_ref, frames_ref, parts_ref, gain_ref, bias_ref, in_ref, res_ref, lo_ref, hi_ref):
    width = frames_ref.shape[1]
    moe = jnp.concatenate(
        [
            parts_ref[2 * q].astype(jnp.float32) + parts_ref[2 * q + 1].astype(jnp.float32)
            for q in range(parts_ref.shape[0] // 2)
        ],
        axis=1,
    )
    residual = frames_ref[...].astype(jnp.float32) + moe
    res_ref[...] = residual
    centered = residual - jnp.mean(residual, axis=1, keepdims=True)
    variance = jnp.mean(centered * centered, axis=1, keepdims=True)
    normed = (centered / jnp.sqrt(variance + 1e-05) * gain_ref[...] + bias_ref[...]).astype(
        jnp.bfloat16
    )
    channels = in_ref.shape[2]
    half = lo_ref.shape[0]
    for n in range(in_ref.shape[0]):
        both = jnp.concatenate([in_ref[n, :width, :], in_ref[n, width : 2 * width, :]], axis=1)
        projected = mm(normed, both)
        glu = projected[:, :channels] * jax.nn.sigmoid(projected[:, channels:])
        glu = glu.astype(jnp.bfloat16)
        cols = slice(n * channels, (n + 1) * channels)
        lo_ref[:, cols] = glu[:half]
        hi_ref[:, cols] = glu[half:]


def conv_kernel(taps, left_ref, lo_ref, hi_ref, right_ref, in_ref, point_ref, res_ref, out_ref, pad_ref):
    half = lo_ref.shape[0]
    count = 2 * half
    for i, ref in enumerate((left_ref, lo_ref, hi_ref, right_ref)):
        pad_ref[i * half : (i + 1) * half, :] = ref[...].astype(jnp.float32)
    base = half - (taps - 1) // 2
    channels = in_ref.shape[2]
    at = 2 * lo_ref.shape[1]
    acts = []
    for n in range(in_ref.shape[0]):
        cols = slice(n * channels, (n + 1) * channels)
        kernel = in_ref[n, at : at + taps + 1, :].astype(jnp.float32)
        total = None
        for j in range(taps):
            term = pad_ref[base + j : base + j + count, cols] * kernel[j : j + 1, :]
            total = term if total is None else total + term
        acts.append((total * jax.nn.sigmoid(total)).astype(jnp.bfloat16))
    act = jnp.concatenate(acts, axis=1)
    out_ref[...] = (res_ref[...] + mm(act, point_ref[...])).astype(jnp.bfloat16)


def shards(
    frames,
    expert_ids,
    gate_values,
    w_gate,
    w_up,
    w_down,
    norm_gain,
    norm_bias,
    point_in,
    depth_kernel,
    point_out,
):
    count, width = frames.shape
    wide = lax.axis_size("x") * lax.axis_size("z")
    quarters, cores = lax.axis_size("y"), lax.axis_size("c")
    narrow = quarters * cores
    experts = w_gate.shape[0] * wide
    slots = 2 * expert_ids.shape[1] * count // experts // cores
    share = width // quarters
    own = count // narrow
    taps, channels = depth_kernel.shape
    params = pltpu.CompilerParams(vmem_limit_bytes=VMEM_BYTES)

    y, c = lax.axis_index("y"), lax.axis_index("c")
    pos = jnp.stack([y, c, y * cores + c]).astype(jnp.int32)

    packed = jnp.concatenate(
        [
            point_in.transpose(1, 0, 2).reshape(2 * width, channels),
            depth_kernel,
            jnp.zeros((1, channels), jnp.bfloat16),
        ],
        axis=0,
    )
    packed = lax.all_gather(packed, NARROW, axis=0)
    point = lax.all_gather(point_out, NARROW, axis=0, tiled=True)

    mine = [w_gate[0], w_up[0], w_down[0]]
    swap = [(i, cores - 1 - i) for i in range(cores)]
    theirs = [lax.ppermute(w, "c", swap) for w in mine]

    rows = experts * slots
    outgoing, target = pl.pallas_call(
        lambda *refs: route_kernel(experts, slots, *refs),
        grid_spec=pltpu.PrefetchScalarGridSpec(
            num_scalar_prefetch=1,
            grid=(1,),
            in_specs=[
                pl.BlockSpec((2, count), lambda i, pos: (0, 0)),
                pl.BlockSpec((count, share), lambda i, pos: (0, pos[0])),
            ],
            out_specs=[
                pl.BlockSpec((rows, share), lambda i, pos: (0, 0)),
                pl.BlockSpec((2, count), lambda i, pos: (0, 0)),
            ],
        ),
        out_shape=[
            jax.ShapeDtypeStruct((rows, share), jnp.bfloat16),
            jax.ShapeDtypeStruct((2, count), jnp.float32),
        ],
        compiler_params=params,
        name="route",
    )(pos, expert_ids.T, frames)

    arrived = lax.all_to_all(
        outgoing.reshape(experts, slots, share), WIDE, split_axis=0, concat_axis=0, tiled=True
    ).reshape(1, rows, share)
    x = lax.all_to_all(
        jnp.broadcast_to(arrived, (quarters, rows, share)), "y", split_axis=0, concat_axis=0, tiled=True
    )
    partial = pl.pallas_call(
        expert_kernel,
        in_specs=in_vmem(7),
        out_specs=pl.BlockSpec(memory_space=pltpu.VMEM),
        out_shape=jax.ShapeDtypeStruct((quarters, rows, share), jnp.bfloat16),
        compiler_params=params,
        name="experts",
    )(x, *mine, *theirs)
    partial = lax.all_to_all(partial, "y", split_axis=0, concat_axis=0, tiled=True)
    summed = jnp.sum(partial.astype(jnp.float32), axis=0).astype(jnp.bfloat16)
    returned = lax.all_to_all(
        summed.reshape(experts, slots, share), WIDE, split_axis=0, concat_axis=0, tiled=True
    ).reshape(rows, share)
    mixed = pl.pallas_call(
        combine_kernel,
        in_specs=in_vmem(3),
        out_specs=pl.BlockSpec(memory_space=pltpu.VMEM),
        out_shape=jax.ShapeDtypeStruct((count, share), jnp.bfloat16),
        compiler_params=params,
        name="combine",
    )(target, gate_values.T, returned)
    parts = lax.all_to_all(
        mixed.reshape(narrow, own, share), NARROW, split_axis=0, concat_axis=0, tiled=True
    )

    half = own // 2
    whole = lambda *shape: pl.BlockSpec(shape, lambda i, pos: (0,) * len(shape))
    residual, lo, hi = pl.pallas_call(
        norm_kernel,
        grid_spec=pltpu.PrefetchScalarGridSpec(
            num_scalar_prefetch=1,
            grid=(1,),
            in_specs=[
                pl.BlockSpec((own, width), lambda i, pos: (pos[2], 0)),
                whole(narrow, own, share),
                whole(1, width),
                whole(1, width),
                whole(*packed.shape),
            ],
            out_specs=[whole(own, width), whole(half, width), whole(half, width)],
        ),
        out_shape=[
            jax.ShapeDtypeStruct((own, width), jnp.float32),
            jax.ShapeDtypeStruct((half, width), jnp.bfloat16),
            jax.ShapeDtypeStruct((half, width), jnp.bfloat16),
        ],
        compiler_params=params,
        name="norm_glu",
    )(pos, frames, parts, norm_gain[None, :], norm_bias[None, :], packed)

    ends = wide * narrow - 1
    left = lax.ppermute(hi, EVERY, [(i, i + 1) for i in range(ends)])
    right = lax.ppermute(lo, EVERY, [(i + 1, i) for i in range(ends)])
    return pl.pallas_call(
        lambda *refs: conv_kernel(taps, *refs),
        in_specs=in_vmem(7),
        out_specs=pl.BlockSpec(memory_space=pltpu.VMEM),
        out_shape=jax.ShapeDtypeStruct((own, width), jnp.bfloat16),
        scratch_shapes=[pltpu.VMEM((4 * half, width), jnp.float32)],
        compiler_params=params,
        name="conv",
    )(left, lo, hi, right, packed, point, residual)


def solution(mesh):
    chips = Mesh(mesh.devices.reshape(4, 16, 4, 2), EVERY)
    return jax.shard_map(
        shards,
        mesh=chips,
        in_specs=(
            P(WIDE, None),
            P(WIDE, None),
            P(WIDE, None),
            P(WIDE, None, NARROW),
            P(WIDE, None, NARROW),
            P(WIDE, NARROW, None),
            P(),
            P(),
            P(None, None, NARROW),
            P(None, NARROW),
            P(NARROW, None),
        ),
        out_specs=P(EVERY, None),
        check_vma=False,
    )
```

```python
import jax
import jax.numpy as jnp
from jax import lax
from jax.experimental import pallas as pl
from jax.experimental.pallas import tpu as pltpu
from jax.sharding import Mesh
from jax.sharding import PartitionSpec as P

WIDE = ("x", "z")
NARROW = ("y", "c")
EVERY = ("x", "z", "y", "c")
VMEM_BYTES = 48 << 20


def in_vmem(count):
    return [pl.BlockSpec(memory_space=pltpu.VMEM)] * count


def mm(a, b):
    return jnp.dot(a, b, preferred_element_type=jnp.float32)


def fetched(copies):
    for copy in copies:
        copy.start()
    return copies


def pack_kernel(in_ref, taps_ref, packed_ref, in_vmem_ref, taps_vmem, wide_ref, sem):
    copies = fetched(
        [
            pltpu.make_async_copy(in_ref, in_vmem_ref, sem.at[0]),
            pltpu.make_async_copy(taps_ref, taps_vmem, sem.at[1]),
        ]
    )
    both, lanes = in_ref.shape
    half = both // 2
    taps = taps_ref.shape[0]
    copies[0].wait()
    wide_ref[...] = in_vmem_ref[...].astype(jnp.float32)
    packed_ref[:half, :] = wide_ref[pl.ds(0, half, 2), :].astype(jnp.bfloat16)
    packed_ref[half:both, :] = wide_ref[pl.ds(1, half, 2), :].astype(jnp.bfloat16)
    copies[1].wait()
    packed_ref[both : both + taps + 1, :] = jnp.concatenate(
        [taps_vmem[...].astype(jnp.float32), jnp.zeros((1, lanes), jnp.float32)], axis=0
    ).astype(jnp.bfloat16)


def route_kernel(experts, slots, ids_ref, frames_ref, out_ref, target_ref, held_ref, ids_vmem, sem):
    count, share = held_ref.shape
    column = pl.multiple_of(lax.axis_index("y") * share, share)
    names, held = fetched(
        [
            pltpu.make_async_copy(ids_ref, ids_vmem, sem.at[0]),
            pltpu.make_async_copy(frames_ref.at[:, pl.ds(column, share)], held_ref, sem.at[1]),
        ]
    )
    names.wait()
    ids = ids_vmem[...]
    first = lax.axis_index("c") * slots
    expert = lax.broadcasted_iota(jnp.int32, (experts, count), 0)
    named = [jnp.where(expert == ids[k : k + 1, :], 1.0, 0.0) for k in range(2)]
    before = lax.broadcasted_iota(jnp.int32, (count, count), 0) < lax.broadcasted_iota(
        jnp.int32, (count, count), 1
    )
    rank = mm(
        jnp.concatenate(named, axis=0).astype(jnp.bfloat16),
        jnp.where(before, 1.0, 0.0).astype(jnp.bfloat16),
    )
    total = jnp.sum(named[0], axis=1, keepdims=True)
    place = [
        jnp.sum(named[0] * rank[:experts], axis=0, keepdims=True),
        jnp.sum(named[1] * (rank[experts:] + total), axis=0, keepdims=True),
    ]
    row = lax.broadcasted_iota(jnp.int32, (experts * slots, count), 0)
    chosen = None
    for k in range(2):
        local = place[k].astype(jnp.int32) - first
        target = jnp.where(
            (local >= 0) & (local < slots), ids[k : k + 1, :] * slots + local, -1
        )
        target_ref[k : k + 1, :] = target.astype(jnp.float32)
        hit = row == target
        chosen = hit if chosen is None else chosen | hit
    pick = jnp.where(chosen, 1.0, 0.0).astype(jnp.bfloat16)
    held.wait()
    out_ref[...] = mm(pick, held_ref[...]).astype(jnp.bfloat16)


def expert_kernel(x_ref, *refs):
    sources, out_ref, held, sem = refs[:6], refs[6], refs[7:13], refs[13]
    order = (0, 1, 3, 4, 2, 5)
    copies = [pltpu.make_async_copy(s, h, sem.at[i]) for i, (s, h) in enumerate(zip(sources, held))]
    for i in order:
        copies[i].start()
    chunks, _, width = x_ref.shape
    hidden = []
    for pair in range(2):
        gate_ref, up_ref = held[3 * pair : 3 * pair + 2]
        x = jnp.concatenate([x_ref[q] for q in range(chunks)], axis=1)
        copies[3 * pair].wait()
        gate = mm(x, gate_ref[...])
        copies[3 * pair + 1].wait()
        up = mm(x, up_ref[...])
        hidden.append((gate * jax.nn.sigmoid(gate) * up).astype(jnp.bfloat16))
    copies[2].wait()
    copies[5].wait()
    for q in range(chunks):
        cols = slice(q * width, (q + 1) * width)
        out_ref[q] = (mm(hidden[0], held[2][:, cols]) + mm(hidden[1], held[5][:, cols])).astype(
            jnp.bfloat16
        )


def combine_kernel(target_ref, gate_ref, rows_ref, out_ref):
    count = target_ref.shape[1]
    table = jnp.concatenate(
        [target_ref[...], gate_ref[...], jnp.zeros((4, count), jnp.float32)], axis=0
    ).T
    slot = lax.broadcasted_iota(jnp.int32, (count, rows_ref.shape[0]), 1)
    total = None
    for k in range(2):
        hit = slot == table[:, k : k + 1].astype(jnp.int32)
        picked = mm(jnp.where(hit, 1.0, 0.0).astype(jnp.bfloat16), rows_ref[...])
        picked = picked * table[:, 2 + k : 3 + k]
        total = picked if total is None else total + picked
    out_ref[...] = total.astype(jnp.bfloat16)


def norm_kernel(
    cores, frames_ref, in_ref, parts_ref, gain_ref, bias_ref, res_ref, lo_ref, hi_ref, taps_ref, own_ref, held_ref, sem
):
    own, width = own_ref.shape
    blocks = in_ref.shape[0]
    index = lax.axis_index("y") * cores + lax.axis_index("c")
    copies = fetched(
        [
            pltpu.make_async_copy(
                frames_ref.at[pl.ds(pl.multiple_of(index * own, own), own), :],
                own_ref,
                sem.at[blocks],
            )
        ]
        + [pltpu.make_async_copy(in_ref.at[n], held_ref.at[n], sem.at[n]) for n in range(blocks)]
    )
    moe = jnp.concatenate(
        [
            parts_ref[2 * q].astype(jnp.float32) + parts_ref[2 * q + 1].astype(jnp.float32)
            for q in range(parts_ref.shape[0] // 2)
        ],
        axis=1,
    )
    copies[0].wait()
    residual = own_ref[...].astype(jnp.float32) + moe
    res_ref[...] = residual
    centered = residual - jnp.mean(residual, axis=1, keepdims=True)
    variance = jnp.mean(centered * centered, axis=1, keepdims=True)
    normed = (centered / jnp.sqrt(variance + 1e-05) * gain_ref[...] + bias_ref[...]).astype(
        jnp.bfloat16
    )
    channels = in_ref.shape[2]
    half = lo_ref.shape[0]
    for n in range(blocks):
        copies[n + 1].wait()
        both = jnp.concatenate(
            [held_ref[n, :width, :], held_ref[n, width : 2 * width, :]], axis=1
        )
        projected = mm(normed, both)
        glu = projected[:, :channels] * jax.nn.sigmoid(projected[:, channels:])
        glu = glu.astype(jnp.bfloat16)
        cols = slice(n * channels, (n + 1) * channels)
        lo_ref[:, cols] = glu[:half]
        hi_ref[:, cols] = glu[half:]
        taps_ref[:, cols] = held_ref[n, 2 * width :, :].astype(jnp.float32)


def conv_kernel(taps, point_ref, left_ref, lo_ref, hi_ref, right_ref, taps_ref, res_ref, out_ref, held_ref, sem):
    half, width = lo_ref.shape
    count = 2 * half
    reach = (taps - 1) // 2
    step = width // sem.shape[0]
    copies = fetched(
        [
            pltpu.make_async_copy(
                point_ref.at[i * step : (i + 1) * step, :],
                held_ref.at[i * step : (i + 1) * step, :],
                sem.at[i],
            )
            for i in range(sem.shape[0])
        ]
    )
    total = res_ref[...]
    for i, copy in enumerate(copies):
        cols = slice(i * step, (i + 1) * step)
        window = jnp.concatenate(
            [ref[:, cols] for ref in (left_ref, lo_ref, hi_ref, right_ref)], axis=0
        ).astype(jnp.float32)
        depth = None
        for turn in range(8):
            moved = pltpu.roll(window, 2 * count - turn, 0) if turn else window
            for j in range(taps):
                start = half - reach + j
                if start % 8 == turn:
                    term = moved[start - turn : start - turn + count] * taps_ref[j : j + 1, cols]
                    depth = term if depth is None else depth + term
        act = (depth * jax.nn.sigmoid(depth)).astype(jnp.bfloat16)
        copy.wait()
        total = total + mm(act, held_ref[cols, :])
    out_ref[...] = total.astype(jnp.bfloat16)


def shards(
    frames,
    expert_ids,
    gate_values,
    w_gate,
    w_up,
    w_down,
    norm_gain,
    norm_bias,
    point_in,
    depth_kernel,
    point_out,
):
    count, width = frames.shape
    wide = lax.axis_size("x") * lax.axis_size("z")
    quarters, cores = lax.axis_size("y"), lax.axis_size("c")
    narrow = quarters * cores
    experts = w_gate.shape[0] * wide
    slots = 2 * expert_ids.shape[1] * count // experts // cores
    share = width // quarters
    own = count // narrow
    taps, channels = depth_kernel.shape
    params = pltpu.CompilerParams(vmem_limit_bytes=VMEM_BYTES)

    in_hbm = lambda n: [pl.BlockSpec(memory_space=pltpu.HBM)] * n
    far = lambda array: pltpu.with_memory_space_constraint(array, pltpu.HBM)
    frames = far(frames)

    packed_rows = 2 * width + taps + 1
    packed = pl.pallas_call(
        pack_kernel,
        in_specs=in_hbm(2),
        out_specs=pl.BlockSpec(memory_space=pltpu.VMEM),
        out_shape=jax.ShapeDtypeStruct((packed_rows, channels), jnp.bfloat16),
        scratch_shapes=[
            pltpu.VMEM((2 * width, channels), jnp.bfloat16),
            pltpu.VMEM((taps, channels), jnp.bfloat16),
            pltpu.VMEM((2 * width, channels), jnp.float32),
            pltpu.SemaphoreType.DMA((2,)),
        ],
        compiler_params=params,
        name="pack",
    )(far(point_in.reshape(2 * width, channels)), far(depth_kernel))
    packed = lax.all_gather(packed, NARROW, axis=0)

    mine = [w_gate[0], w_up[0], w_down[0]]
    swap = [(i, cores - 1 - i) for i in range(cores)]
    theirs = [lax.ppermute(w, "c", swap) for w in mine]

    rows = experts * slots
    outgoing, target = pl.pallas_call(
        lambda *refs: route_kernel(experts, slots, *refs),
        in_specs=in_hbm(2),
        out_specs=in_vmem(2),
        out_shape=[
            jax.ShapeDtypeStruct((rows, share), jnp.bfloat16),
            jax.ShapeDtypeStruct((2, count), jnp.float32),
        ],
        scratch_shapes=[
            pltpu.VMEM((count, share), jnp.bfloat16),
            pltpu.VMEM((2, count), jnp.int32),
            pltpu.SemaphoreType.DMA((2,)),
        ],
        compiler_params=params,
        name="route",
    )(far(expert_ids.T), frames)

    def over(axis, cells):
        return lax.all_to_all(cells, axis, split_axis=0, concat_axis=0, tiled=True)

    arrived = over(WIDE, outgoing.reshape(experts, slots, share)).reshape(1, rows, share)
    x = over("y", jnp.broadcast_to(arrived, (quarters, rows, share)))
    weights = mine + theirs
    partial = pl.pallas_call(
        expert_kernel,
        in_specs=in_vmem(1) + in_hbm(6),
        out_specs=pl.BlockSpec(memory_space=pltpu.VMEM),
        out_shape=jax.ShapeDtypeStruct((quarters, rows, share), jnp.bfloat16),
        scratch_shapes=[pltpu.VMEM(w.shape, w.dtype) for w in weights]
        + [pltpu.SemaphoreType.DMA((6,))],
        compiler_params=params,
        name="experts",
    )(x, *[far(w) for w in weights])
    partial = over("y", partial)
    summed = jnp.sum(partial.astype(jnp.float32), axis=0).astype(jnp.bfloat16)
    summed, point_out = lax.optimization_barrier((summed, point_out))
    point = lax.all_gather(point_out, NARROW, axis=0, tiled=True)
    returned = over(WIDE, summed.reshape(experts, slots, share)).reshape(rows, share)
    mixed = pl.pallas_call(
        combine_kernel,
        in_specs=in_vmem(3),
        out_specs=pl.BlockSpec(memory_space=pltpu.VMEM),
        out_shape=jax.ShapeDtypeStruct((count, share), jnp.bfloat16),
        compiler_params=params,
        name="combine",
    )(target, gate_values.T, returned)
    parts = over(NARROW, mixed.reshape(narrow, own, share))

    half = own // 2
    residual, lo, hi, kernel = pl.pallas_call(
        lambda *refs: norm_kernel(cores, *refs),
        in_specs=in_hbm(2) + in_vmem(3),
        out_specs=in_vmem(4),
        out_shape=[
            jax.ShapeDtypeStruct((own, width), jnp.float32),
            jax.ShapeDtypeStruct((half, width), jnp.bfloat16),
            jax.ShapeDtypeStruct((half, width), jnp.bfloat16),
            jax.ShapeDtypeStruct((taps + 1, width), jnp.float32),
        ],
        scratch_shapes=[
            pltpu.VMEM((own, width), jnp.bfloat16),
            pltpu.VMEM(packed.shape, jnp.bfloat16),
            pltpu.SemaphoreType.DMA((narrow + 1,)),
        ],
        compiler_params=params,
        name="norm_glu",
    )(frames, far(packed), parts, norm_gain[None, :], norm_bias[None, :])

    ends = wide * narrow - 1
    left = lax.ppermute(hi, EVERY, [(i, i + 1) for i in range(ends)])
    right = lax.ppermute(lo, EVERY, [(i + 1, i) for i in range(ends)])
    return pl.pallas_call(
        lambda *refs: conv_kernel(taps, *refs),
        in_specs=in_hbm(1) + in_vmem(6),
        out_specs=pl.BlockSpec(memory_space=pltpu.VMEM),
        out_shape=jax.ShapeDtypeStruct((own, width), jnp.bfloat16),
        scratch_shapes=[
            pltpu.VMEM((width, width), jnp.bfloat16),
            pltpu.SemaphoreType.DMA((quarters,)),
        ],
        compiler_params=params,
        name="conv",
    )(far(point), left, lo, hi, right, kernel, residual)


def solution(mesh):
    chips = Mesh(mesh.devices.reshape(4, 16, 4, 2), EVERY)
    return jax.shard_map(
        shards,
        mesh=chips,
        in_specs=(
            P(WIDE, None),
            P(WIDE, None),
            P(WIDE, None),
            P(WIDE, None, NARROW),
            P(WIDE, None, NARROW),
            P(WIDE, NARROW, None),
            P(),
            P(),
            P(None, None, NARROW),
            P(None, NARROW),
            P(NARROW, None),
        ),
        out_specs=P(EVERY, None),
        check_vma=False,
    )
```

```python
import jax
import jax.numpy as jnp
from jax import lax
from jax.experimental import pallas as pl
from jax.experimental.pallas import tpu as pltpu
from jax.sharding import Mesh
from jax.sharding import PartitionSpec as P

WIDE = ("x", "z")
NARROW = ("y", "c")
EVERY = ("x", "z", "y", "c")
VMEM_BYTES = 32 << 20


def in_vmem(count):
    return [pl.BlockSpec(memory_space=pltpu.VMEM)] * count


def mm(a, b):
    return jnp.dot(a, b, preferred_element_type=jnp.float32)


def fetched(copies):
    for copy in copies:
        copy.start()
    return copies


def prepare_kernel(
    experts,
    slots,
    ids_ref,
    frames_ref,
    in_ref,
    taps_ref,
    point_ref,
    gates_ref,
    out_ref,
    table_ref,
    packed_ref,
    held_ref,
    ids_vmem,
    gates_vmem,
    in_vmem_ref,
    taps_vmem,
    wide_ref,
    sem,
):
    both, lanes = in_ref.shape
    half = both // 2
    taps = taps_ref.shape[0]
    at = both + taps + 1
    count, share = held_ref.shape
    column = pl.multiple_of(lax.axis_index("y") * share, share)
    names, held, halves, kernel, gates, *points = fetched(
        [
            pltpu.make_async_copy(ids_ref, ids_vmem, sem.at[0]),
            pltpu.make_async_copy(frames_ref.at[:, pl.ds(column, share)], held_ref, sem.at[1]),
            pltpu.make_async_copy(in_ref, in_vmem_ref, sem.at[2]),
            pltpu.make_async_copy(taps_ref, taps_vmem, sem.at[3]),
            pltpu.make_async_copy(gates_ref, gates_vmem, sem.at[4]),
        ]
        + [
            pltpu.make_async_copy(
                point_ref.at[:, b * lanes : (b + 1) * lanes],
                packed_ref.at[at + b * lanes : at + (b + 1) * lanes, :],
                sem.at[5 + b],
            )
            for b in range(point_ref.shape[1] // lanes)
        ]
    )
    names.wait()
    ids = ids_vmem[...]
    first = lax.axis_index("c") * slots
    expert = lax.broadcasted_iota(jnp.int32, (experts, count), 0)
    named = [jnp.where(expert == ids[k : k + 1, :], 1.0, 0.0) for k in range(2)]
    before = lax.broadcasted_iota(jnp.int32, (count, count), 0) < lax.broadcasted_iota(
        jnp.int32, (count, count), 1
    )
    rank = mm(
        jnp.concatenate(named, axis=0).astype(jnp.bfloat16),
        jnp.where(before, 1.0, 0.0).astype(jnp.bfloat16),
    )
    total = jnp.sum(named[0], axis=1, keepdims=True)
    place = [
        jnp.sum(named[0] * rank[:experts], axis=0, keepdims=True),
        jnp.sum(named[1] * (rank[experts:] + total), axis=0, keepdims=True),
    ]
    row = lax.broadcasted_iota(jnp.int32, (experts * slots, count), 0)
    chosen = None
    targets = []
    for k in range(2):
        local = place[k].astype(jnp.int32) - first
        target = jnp.where(
            (local >= 0) & (local < slots), ids[k : k + 1, :] * slots + local, -1
        )
        targets.append(target.astype(jnp.float32))
        hit = row == target
        chosen = hit if chosen is None else chosen | hit
    pick = jnp.where(chosen, 1.0, 0.0).astype(jnp.bfloat16)
    held.wait()
    out_ref[...] = mm(pick, held_ref[...]).astype(jnp.bfloat16)
    halves.wait()
    wide_ref[...] = in_vmem_ref[...].astype(jnp.float32)
    packed_ref[:half, :] = wide_ref[pl.ds(0, half, 2), :].astype(jnp.bfloat16)
    packed_ref[half:both, :] = wide_ref[pl.ds(1, half, 2), :].astype(jnp.bfloat16)
    kernel.wait()
    packed_ref[both:at, :] = jnp.concatenate(
        [taps_vmem[...].astype(jnp.float32), jnp.zeros((1, lanes), jnp.float32)], axis=0
    ).astype(jnp.bfloat16)
    gates.wait()
    table_ref[...] = jnp.concatenate(
        targets + [gates_vmem[...], jnp.zeros((4, count), jnp.float32)], axis=0
    )
    for copy in points:
        copy.wait()


def expert_kernel(x_ref, *refs):
    sources, out_ref, held, sem = refs[:6], refs[6], refs[7:13], refs[13]
    chunks, _, width = x_ref.shape
    units = held[0].shape[1]
    parts = [slice(i * width, (i + 1) * width) for i in range(units // width)]
    loads = {}
    for pair in range(2):
        for i, cols in enumerate(parts):
            for which in (3 * pair, 3 * pair + 1):
                at = sem.at[len(loads)]
                loads[which, i] = pltpu.make_async_copy(
                    sources[which].at[:, cols], held[which].at[:, cols], at
                )
    for which in (2, 5):
        loads[which, 0] = pltpu.make_async_copy(sources[which], held[which], sem.at[len(loads)])
    for copy in loads.values():
        copy.start()
    x = jnp.concatenate([x_ref[q] for q in range(chunks)], axis=1)
    hidden = []
    for pair in range(2):
        for i, cols in enumerate(parts):
            loads[3 * pair, i].wait()
            gate = mm(x, held[3 * pair][:, cols])
            loads[3 * pair + 1, i].wait()
            up = mm(x, held[3 * pair + 1][:, cols])
            hidden.append((gate * jax.nn.sigmoid(gate) * up).astype(jnp.bfloat16))
    hidden = jnp.concatenate(hidden, axis=1)
    loads[2, 0].wait()
    loads[5, 0].wait()
    for q in range(chunks):
        cols = slice(q * width, (q + 1) * width)
        total = mm(hidden[:, :units], held[2][:, cols]) + mm(hidden[:, units:], held[5][:, cols])
        out_ref[q] = total.astype(jnp.bfloat16)


def gather(quarters, cores, first, last, sources, out_ref, sem):
    y, c = lax.axis_index("y"), lax.axis_index("c")
    rows, cut = sources[0].shape[0], sources[3].shape[0]
    copies, order = {}, []
    for side in range(2):
        core = c if side == 0 else cores - 1 - c
        for i, (shift, start, stop) in enumerate(
            ((0, 0, rows), (quarters - 1, 0, rows), (1, 0, rows), (2, 0, cut), (2, cut, rows))
        ):
            block = 4 * side + min(i, 3)
            if block == len(order):
                order.append(lax.rem(y + shift, quarters) * cores + core)
                copies[block] = []
            low, high = max(first, start), min(last, stop)
            if low < high:
                copies[block].append(
                    pltpu.make_async_copy(
                        sources[5 * side + i].at[low - start : high - start, :],
                        out_ref.at[block, low - first : high - first, :],
                        sem.at[5 * side + i],
                    )
                )
                copies[block][-1].start()
    return copies, order


def combine_kernel(table_ref, rows_ref, out_ref):
    count = table_ref.shape[1]
    table = table_ref[...].T
    slot = lax.broadcasted_iota(jnp.int32, (count, rows_ref.shape[0]), 1)
    total = None
    for k in range(2):
        hit = slot == table[:, k : k + 1].astype(jnp.int32)
        picked = mm(jnp.where(hit, 1.0, 0.0).astype(jnp.bfloat16), rows_ref[...])
        picked = picked * table[:, 2 + k : 3 + k]
        total = picked if total is None else total + picked
    out_ref[...] = total.astype(jnp.bfloat16)


def norm_kernel(quarters, cores, frames_ref, *refs):
    parts_ref, gain_ref, bias_ref, res_ref, lo_ref, hi_ref, taps_ref, own_ref, held_ref, sem = refs[10:]
    own, width = own_ref.shape
    index = lax.axis_index("y") * cores + lax.axis_index("c")
    fetch = pltpu.make_async_copy(
        frames_ref.at[pl.ds(pl.multiple_of(index * own, own), own), :], own_ref, sem.at[10]
    )
    fetch.start()
    copies, order = gather(quarters, cores, 0, held_ref.shape[1], refs[:10], held_ref, sem)
    moe = jnp.concatenate(
        [
            parts_ref[2 * q].astype(jnp.float32) + parts_ref[2 * q + 1].astype(jnp.float32)
            for q in range(parts_ref.shape[0] // 2)
        ],
        axis=1,
    )
    fetch.wait()
    residual = own_ref[...].astype(jnp.float32) + moe
    res_ref[...] = residual
    centered = residual - jnp.mean(residual, axis=1, keepdims=True)
    variance = jnp.mean(centered * centered, axis=1, keepdims=True)
    normed = (centered / jnp.sqrt(variance + 1e-05) * gain_ref[...] + bias_ref[...]).astype(
        jnp.bfloat16
    )
    channels = held_ref.shape[2]
    half = lo_ref.shape[0]
    for block, index in enumerate(order):
        for copy in copies[block]:
            copy.wait()
        both = jnp.concatenate(
            [held_ref[block, :width, :], held_ref[block, width : 2 * width, :]], axis=1
        )
        projected = mm(normed, both)
        glu = projected[:, :channels] * jax.nn.sigmoid(projected[:, channels:])
        glu = glu.astype(jnp.bfloat16)
        cols = pl.ds(pl.multiple_of(index * channels, channels), channels)
        lo_ref[:, cols] = glu[:half]
        hi_ref[:, cols] = glu[half:]
        taps_ref[:, cols] = held_ref[block, 2 * width :, :].astype(jnp.float32)


def conv_kernel(quarters, cores, taps, *refs):
    left_ref, lo_ref, hi_ref, right_ref, taps_ref, res_ref, out_ref, act_ref, held_ref, sem = refs[10:]
    blocks, rows, channels = held_ref.shape
    last = refs[0].shape[0]
    copies, order = gather(quarters, cores, last - rows, last, refs[:10], held_ref, sem)
    half, width = lo_ref.shape
    count = 2 * half
    reach = (taps - 1) // 2
    for n in range(0, blocks, 2):
        cols = slice(n * channels, (n + 2) * channels)
        window = jnp.concatenate(
            [ref[:, cols] for ref in (left_ref, lo_ref, hi_ref, right_ref)], axis=0
        ).astype(jnp.float32)
        depth = None
        for turn in range(8):
            moved = pltpu.roll(window, 2 * count - turn, 0) if turn else window
            for j in range(taps):
                start = half - reach + j
                if start % 8 == turn:
                    term = moved[start - turn : start - turn + count] * taps_ref[j : j + 1, cols]
                    depth = term if depth is None else depth + term
        act_ref[:, cols] = (depth * jax.nn.sigmoid(depth)).astype(jnp.bfloat16)
    acts, points = [], []
    for block, index in enumerate(order):
        for copy in copies[block]:
            copy.wait()
        acts.append(act_ref[:, pl.ds(pl.multiple_of(index * channels, channels), channels)])
        points.append(
            jnp.concatenate(
                [held_ref[block, b * channels : (b + 1) * channels, :] for b in range(blocks)],
                axis=1,
            )
        )
    total = res_ref[...] + mm(jnp.concatenate(acts, axis=1), jnp.concatenate(points, axis=0))
    out_ref[...] = total.astype(jnp.bfloat16)


def shards(
    frames,
    expert_ids,
    gate_values,
    w_gate,
    w_up,
    w_down,
    norm_gain,
    norm_bias,
    point_in,
    depth_kernel,
    point_out,
):
    count, width = frames.shape
    wide = lax.axis_size("x") * lax.axis_size("z")
    quarters, cores = lax.axis_size("y"), lax.axis_size("c")
    narrow = quarters * cores
    experts = w_gate.shape[0] * wide
    slots = 2 * expert_ids.shape[1] * count // experts // cores
    share = width // quarters
    own = count // narrow
    taps, channels = depth_kernel.shape
    params = pltpu.CompilerParams(vmem_limit_bytes=VMEM_BYTES)

    in_hbm = lambda n: [pl.BlockSpec(memory_space=pltpu.HBM)] * n
    far = lambda array: pltpu.with_memory_space_constraint(array, pltpu.HBM)
    frames = far(frames)

    mine = [w_gate[0], w_up[0], w_down[0]]
    swap = [(i, cores - 1 - i) for i in range(cores)]
    theirs = [lax.ppermute(w, "c", swap) for w in mine]

    rows = experts * slots
    packed_rows = 3 * width + taps + 1
    outgoing, table, packed = pl.pallas_call(
        lambda *refs: prepare_kernel(experts, slots, *refs),
        in_specs=in_hbm(6),
        out_specs=in_vmem(3),
        out_shape=[
            jax.ShapeDtypeStruct((rows, share), jnp.bfloat16),
            jax.ShapeDtypeStruct((8, count), jnp.float32),
            jax.ShapeDtypeStruct((packed_rows, channels), jnp.bfloat16),
        ],
        scratch_shapes=[
            pltpu.VMEM((count, share), jnp.bfloat16),
            pltpu.VMEM((2, count), jnp.int32),
            pltpu.VMEM((2, count), jnp.float32),
            pltpu.VMEM((2 * width, channels), jnp.bfloat16),
            pltpu.VMEM((taps, channels), jnp.bfloat16),
            pltpu.VMEM((2 * width, channels), jnp.float32),
            pltpu.SemaphoreType.DMA((5 + narrow,)),
        ],
        compiler_params=params,
        name="prepare",
    )(
        far(expert_ids.T),
        frames,
        far(point_in.reshape(2 * width, channels)),
        far(depth_kernel),
        far(point_out),
        far(gate_values.T),
    )

    ahead = [(i, (i + 1) % quarters) for i in range(quarters)]
    behind = [((i + 1) % quarters, i) for i in range(quarters)]
    before = lax.ppermute(packed, "y", ahead)
    after = lax.ppermute(packed, "y", behind)

    def over(axis, cells):
        return lax.all_to_all(cells, axis, split_axis=0, concat_axis=0, tiled=True)

    arrived = over(WIDE, outgoing.reshape(experts, slots, share)).reshape(1, rows, share)
    x = over("y", jnp.broadcast_to(arrived, (quarters, rows, share)))
    weights = mine + theirs
    partial = pl.pallas_call(
        expert_kernel,
        in_specs=in_vmem(1) + in_hbm(6),
        out_specs=pl.BlockSpec(memory_space=pltpu.VMEM),
        out_shape=jax.ShapeDtypeStruct((quarters, rows, share), jnp.bfloat16),
        scratch_shapes=[pltpu.VMEM(w.shape, w.dtype) for w in weights]
        + [pltpu.SemaphoreType.DMA((4 * w_gate.shape[2] // share + 2,))],
        compiler_params=params,
        name="experts",
    )(x, *[far(w) for w in weights])
    partial = over("y", partial)
    summed = jnp.sum(partial.astype(jnp.float32), axis=0).astype(jnp.bfloat16)
    summed, packed, before, after = lax.optimization_barrier((summed, packed, before, after))
    cut = packed_rows // 2
    held = [
        packed,
        before,
        after,
        lax.ppermute(before[:cut], "y", ahead),
        lax.ppermute(after[cut:], "y", behind),
    ]
    held = held + [lax.ppermute(cells, "c", swap) for cells in held]
    returned = over(WIDE, summed.reshape(experts, slots, share)).reshape(rows, share)
    mixed = pl.pallas_call(
        combine_kernel,
        in_specs=in_vmem(2),
        out_specs=pl.BlockSpec(memory_space=pltpu.VMEM),
        out_shape=jax.ShapeDtypeStruct((count, share), jnp.bfloat16),
        compiler_params=params,
        name="combine",
    )(table, returned)
    held = [far(cells) for cells in held]
    parts = over(NARROW, mixed.reshape(narrow, own, share))

    half = own // 2
    residual, lo, hi, kernel = pl.pallas_call(
        lambda *refs: norm_kernel(quarters, cores, *refs),
        in_specs=in_hbm(11) + in_vmem(3),
        out_specs=in_vmem(4),
        out_shape=[
            jax.ShapeDtypeStruct((own, width), jnp.float32),
            jax.ShapeDtypeStruct((half, width), jnp.bfloat16),
            jax.ShapeDtypeStruct((half, width), jnp.bfloat16),
            jax.ShapeDtypeStruct((taps + 1, width), jnp.float32),
        ],
        scratch_shapes=[
            pltpu.VMEM((own, width), jnp.bfloat16),
            pltpu.VMEM((narrow, packed_rows - width, channels), jnp.bfloat16),
            pltpu.SemaphoreType.DMA((11,)),
        ],
        compiler_params=params,
        name="norm_glu",
    )(frames, *held, parts, norm_gain[None, :], norm_bias[None, :])

    ends = wide * narrow - 1
    left = lax.ppermute(hi, EVERY, [(i, i + 1) for i in range(ends)])
    right = lax.ppermute(lo, EVERY, [(i + 1, i) for i in range(ends)])
    return pl.pallas_call(
        lambda *refs: conv_kernel(quarters, cores, taps, *refs),
        in_specs=in_hbm(10) + in_vmem(6),
        out_specs=pl.BlockSpec(memory_space=pltpu.VMEM),
        out_shape=jax.ShapeDtypeStruct((own, width), jnp.bfloat16),
        scratch_shapes=[
            pltpu.VMEM((own, width), jnp.bfloat16),
            pltpu.VMEM((narrow, width, channels), jnp.bfloat16),
            pltpu.SemaphoreType.DMA((10,)),
        ],
        compiler_params=params,
        name="conv",
    )(*held, left, lo, hi, right, kernel, residual)


def solution(mesh):
    chips = Mesh(mesh.devices.reshape(4, 16, 4, 2), EVERY)
    return jax.shard_map(
        shards,
        mesh=chips,
        in_specs=(
            P(WIDE, None),
            P(WIDE, None),
            P(WIDE, None),
            P(WIDE, None, NARROW),
            P(WIDE, None, NARROW),
            P(WIDE, NARROW, None),
            P(),
            P(),
            P(None, None, NARROW),
            P(None, NARROW),
            P(NARROW, None),
        ),
        out_specs=P(EVERY, None),
        check_vma=False,
    )
```

```python
import jax
import jax.numpy as jnp
from jax import lax
from jax.experimental import pallas as pl
from jax.experimental.pallas import tpu as pltpu
from jax.sharding import Mesh
from jax.sharding import PartitionSpec as P

WIDE = ("x", "z")
NARROW = ("y", "c")
EVERY = ("x", "z", "y", "c")
VMEM_BYTES = 24 << 20


def in_vmem(count):
    return [pl.BlockSpec(memory_space=pltpu.VMEM)] * count


def mm(a, b):
    return jnp.dot(a, b, preferred_element_type=jnp.float32)


def fetched(copies):
    for copy in copies:
        copy.start()
    return copies


def prepare_kernel(
    experts,
    slots,
    ids_ref,
    frames_ref,
    in_ref,
    taps_ref,
    point_ref,
    gates_ref,
    out_ref,
    table_ref,
    packed_ref,
    held_ref,
    ids_vmem,
    gates_vmem,
    in_vmem_ref,
    taps_vmem,
    wide_ref,
    sem,
):
    both, lanes = in_ref.shape
    half = both // 2
    taps = taps_ref.shape[0]
    at = both + taps + 1
    count, share = held_ref.shape
    column = pl.multiple_of(lax.axis_index("y") * share, share)
    names, held, halves, kernel, gates, *points = fetched(
        [
            pltpu.make_async_copy(ids_ref, ids_vmem, sem.at[0]),
            pltpu.make_async_copy(frames_ref.at[:, pl.ds(column, share)], held_ref, sem.at[1]),
            pltpu.make_async_copy(in_ref, in_vmem_ref, sem.at[2]),
            pltpu.make_async_copy(taps_ref, taps_vmem, sem.at[3]),
            pltpu.make_async_copy(gates_ref, gates_vmem, sem.at[4]),
        ]
        + [
            pltpu.make_async_copy(
                point_ref.at[:, b * lanes : (b + 1) * lanes],
                packed_ref.at[at + b * lanes : at + (b + 1) * lanes, :],
                sem.at[5 + b],
            )
            for b in range(point_ref.shape[1] // lanes)
        ]
    )
    names.wait()
    ids = ids_vmem[...]
    first = lax.axis_index("c") * slots
    expert = lax.broadcasted_iota(jnp.int32, (experts, count), 0)
    named = [jnp.where(expert == ids[k : k + 1, :], 1.0, 0.0) for k in range(2)]
    before = lax.broadcasted_iota(jnp.int32, (count, count), 0) < lax.broadcasted_iota(
        jnp.int32, (count, count), 1
    )
    rank = mm(
        jnp.concatenate(named, axis=0).astype(jnp.bfloat16),
        jnp.where(before, 1.0, 0.0).astype(jnp.bfloat16),
    )
    total = jnp.sum(named[0], axis=1, keepdims=True)
    place = [
        jnp.sum(named[0] * rank[:experts], axis=0, keepdims=True),
        jnp.sum(named[1] * (rank[experts:] + total), axis=0, keepdims=True),
    ]
    row = lax.broadcasted_iota(jnp.int32, (experts * slots, count), 0)
    chosen = None
    targets = []
    for k in range(2):
        local = place[k].astype(jnp.int32) - first
        target = jnp.where(
            (local >= 0) & (local < slots), ids[k : k + 1, :] * slots + local, -1
        )
        targets.append(target.astype(jnp.float32))
        hit = row == target
        chosen = hit if chosen is None else chosen | hit
    pick = jnp.where(chosen, 1.0, 0.0).astype(jnp.bfloat16)
    held.wait()
    out_ref[...] = mm(pick, held_ref[...]).astype(jnp.bfloat16)
    halves.wait()
    wide_ref[...] = in_vmem_ref[...].astype(jnp.float32)
    packed_ref[:half, :] = wide_ref[pl.ds(0, half, 2), :].astype(jnp.bfloat16)
    packed_ref[half:both, :] = wide_ref[pl.ds(1, half, 2), :].astype(jnp.bfloat16)
    kernel.wait()
    packed_ref[both:at, :] = jnp.concatenate(
        [taps_vmem[...].astype(jnp.float32), jnp.zeros((1, lanes), jnp.float32)], axis=0
    ).astype(jnp.bfloat16)
    gates.wait()
    table_ref[...] = jnp.concatenate(
        targets + [gates_vmem[...], jnp.zeros((4, count), jnp.float32)], axis=0
    )
    for copy in points:
        copy.wait()


def expert_kernel(x_ref, *refs):
    sources, out_ref, held, sem = refs[:6], refs[6], refs[7:13], refs[13]
    copies = [pltpu.make_async_copy(s, h, sem.at[i]) for i, (s, h) in enumerate(zip(sources, held))]
    for i in (0, 1, 3, 4, 2, 5):
        copies[i].start()
    chunks, _, width = x_ref.shape
    x = jnp.concatenate([x_ref[q] for q in range(chunks)], axis=1)
    hidden = []
    for pair in range(2):
        copies[3 * pair].wait()
        gate = mm(x, held[3 * pair][...])
        copies[3 * pair + 1].wait()
        up = mm(x, held[3 * pair + 1][...])
        hidden.append((gate * jax.nn.sigmoid(gate) * up).astype(jnp.bfloat16))
    copies[2].wait()
    copies[5].wait()
    for q in range(chunks):
        cols = slice(q * width, (q + 1) * width)
        out_ref[q] = (mm(hidden[0], held[2][:, cols]) + mm(hidden[1], held[5][:, cols])).astype(
            jnp.bfloat16
        )


def blocks_of(quarters, cores, near):
    y, c = lax.axis_index("y"), lax.axis_index("c")
    index = [
        lax.rem(y + (2 * side - 1) * step + quarters, quarters) * cores + side
        for side in (c, cores - 1 - c)
        for step in range(quarters)
    ]
    return [index[i] for i in order_of(len(index), near)]


def order_of(count, near):
    return [i for i in range(count) if i in near] + [i for i in range(count) if i not in near]


def fetched_rows(near, first, last, refs, held_ref, sem):
    views = [(ref.at[first:last, :], None) for ref in refs[: len(near)]]
    for i, ref in enumerate(refs[len(near) :]):
        copy = pltpu.make_async_copy(ref.at[first:last, :], held_ref.at[i], sem.at[i])
        copy.start()
        views.append((held_ref.at[i], copy))
    return views


def combine_kernel(table_ref, rows_ref, out_ref):
    count = table_ref.shape[1]
    table = table_ref[...].T
    slot = lax.broadcasted_iota(jnp.int32, (count, rows_ref.shape[0]), 1)
    total = None
    for k in range(2):
        hit = slot == table[:, k : k + 1].astype(jnp.int32)
        picked = mm(jnp.where(hit, 1.0, 0.0).astype(jnp.bfloat16), rows_ref[...])
        picked = picked * table[:, 2 + k : 3 + k]
        total = picked if total is None else total + picked
    out_ref[...] = total.astype(jnp.bfloat16)


def norm_kernel(quarters, cores, near, frames_ref, *refs):
    count = quarters * cores
    parts_ref, gain_ref, bias_ref, res_ref, lo_ref, hi_ref, taps_ref, own_ref, held_ref, sem = refs[count:]
    own, width = own_ref.shape
    index = lax.axis_index("y") * cores + lax.axis_index("c")
    fetch = pltpu.make_async_copy(
        frames_ref.at[pl.ds(pl.multiple_of(index * own, own), own), :], own_ref, sem.at[count]
    )
    fetch.start()
    views = fetched_rows(near, 0, held_ref.shape[1], refs[:count], held_ref, sem)
    moe = jnp.concatenate(
        [
            parts_ref[2 * q].astype(jnp.float32) + parts_ref[2 * q + 1].astype(jnp.float32)
            for q in range(parts_ref.shape[0] // 2)
        ],
        axis=1,
    )
    fetch.wait()
    residual = own_ref[...].astype(jnp.float32) + moe
    res_ref[...] = residual
    centered = residual - jnp.mean(residual, axis=1, keepdims=True)
    variance = jnp.mean(centered * centered, axis=1, keepdims=True)
    normed = (centered / jnp.sqrt(variance + 1e-05) * gain_ref[...] + bias_ref[...]).astype(
        jnp.bfloat16
    )
    channels = width // count
    half, taps = lo_ref.shape[0], taps_ref.shape[0]
    for (ref, copy), index in zip(views, blocks_of(quarters, cores, near)):
        if copy is not None:
            copy.wait()
        both = jnp.concatenate([ref[:width, :], ref[width : 2 * width, :]], axis=1)
        projected = mm(normed, both)
        glu = projected[:, :channels] * jax.nn.sigmoid(projected[:, channels:])
        glu = glu.astype(jnp.bfloat16)
        cols = pl.ds(pl.multiple_of(index * channels, channels), channels)
        lo_ref[:, cols] = glu[:half]
        hi_ref[:, cols] = glu[half:]
        taps_ref[:, cols] = ref[2 * width : 2 * width + taps, :].astype(jnp.float32)


def conv_kernel(quarters, cores, near, taps, *refs):
    blocks = quarters * cores
    left_ref, lo_ref, hi_ref, right_ref, taps_ref, res_ref, out_ref, act_ref, held_ref, sem = refs[blocks:]
    half, width = lo_ref.shape
    count = 2 * half
    reach = (taps - 1) // 2
    channels = width // blocks
    first = 2 * width + taps + 1
    views = fetched_rows(near, first, first + width, refs[:blocks], held_ref, sem)
    for n in range(0, blocks, 2):
        cols = slice(n * channels, (n + 2) * channels)
        window = jnp.concatenate(
            [ref[:, cols] for ref in (left_ref, lo_ref, hi_ref, right_ref)], axis=0
        ).astype(jnp.float32)
        depth = None
        for turn in range(8):
            moved = pltpu.roll(window, 2 * count - turn, 0) if turn else window
            for j in range(taps):
                start = half - reach + j
                if start % 8 == turn:
                    term = moved[start - turn : start - turn + count] * taps_ref[j : j + 1, cols]
                    depth = term if depth is None else depth + term
        act_ref[:, cols] = (depth * jax.nn.sigmoid(depth)).astype(jnp.bfloat16)
    acts, points = [], []
    for (ref, copy), index in zip(views, blocks_of(quarters, cores, near)):
        if copy is not None:
            copy.wait()
        acts.append(act_ref[:, pl.ds(pl.multiple_of(index * channels, channels), channels)])
        points.append(
            jnp.concatenate(
                [ref[b * channels : (b + 1) * channels, :] for b in range(blocks)],
                axis=1,
            )
        )
    total = res_ref[...] + mm(jnp.concatenate(acts, axis=1), jnp.concatenate(points, axis=0))
    out_ref[...] = total.astype(jnp.bfloat16)


def shards(
    frames,
    expert_ids,
    gate_values,
    w_gate,
    w_up,
    w_down,
    norm_gain,
    norm_bias,
    point_in,
    depth_kernel,
    point_out,
):
    count, width = frames.shape
    wide = lax.axis_size("x") * lax.axis_size("z")
    quarters, cores = lax.axis_size("y"), lax.axis_size("c")
    narrow = quarters * cores
    experts = w_gate.shape[0] * wide
    slots = 2 * expert_ids.shape[1] * count // experts // cores
    share = width // quarters
    own = count // narrow
    taps, channels = depth_kernel.shape
    params = pltpu.CompilerParams(vmem_limit_bytes=VMEM_BYTES)

    in_hbm = lambda n: [pl.BlockSpec(memory_space=pltpu.HBM)] * n
    far = lambda array: pltpu.with_memory_space_constraint(array, pltpu.HBM)
    frames = far(frames)

    rows = experts * slots
    packed_rows = 3 * width + taps + 1
    outgoing, table, packed = pl.pallas_call(
        lambda *refs: prepare_kernel(experts, slots, *refs),
        in_specs=in_hbm(6),
        out_specs=in_vmem(3),
        out_shape=[
            jax.ShapeDtypeStruct((rows, share), jnp.bfloat16),
            jax.ShapeDtypeStruct((8, count), jnp.float32),
            jax.ShapeDtypeStruct((packed_rows, channels), jnp.bfloat16),
        ],
        scratch_shapes=[
            pltpu.VMEM((count, share), jnp.bfloat16),
            pltpu.VMEM((2, count), jnp.int32),
            pltpu.VMEM((2, count), jnp.float32),
            pltpu.VMEM((2 * width, channels), jnp.bfloat16),
            pltpu.VMEM((taps, channels), jnp.bfloat16),
            pltpu.VMEM((2 * width, channels), jnp.float32),
            pltpu.SemaphoreType.DMA((5 + narrow,)),
        ],
        compiler_params=params,
        name="prepare",
    )(
        far(expert_ids.T),
        frames,
        far(point_in.reshape(2 * width, channels)),
        far(depth_kernel),
        far(point_out),
        far(gate_values.T),
    )

    ring = [
        (y * cores + c, (y + 1 - 2 * c) % quarters * cores + c)
        for y in range(quarters)
        for c in range(cores)
    ]
    swap = [(i, cores - 1 - i) for i in range(cores)]
    around = lambda cells: lax.ppermute(cells, NARROW, ring)
    across = lambda cells: lax.ppermute(cells, "c", swap)
    held = [packed]
    for _ in range(quarters - 2):
        held.append(around(held[-1]))

    def over(axis, cells):
        return lax.all_to_all(cells, axis, split_axis=0, concat_axis=0, tiled=True)

    arrived = over(WIDE, outgoing.reshape(experts, slots, share)).reshape(1, rows, share)
    mine = [w_gate[0], w_up[0], w_down[0]]
    theirs = [across(w) for w in mine]
    arrived, *held = lax.optimization_barrier((arrived, *held))
    swapped = [across(cells) for cells in held]
    held.append(around(held[-1]))
    x = over("y", jnp.broadcast_to(arrived, (quarters, rows, share)))
    weights = mine + theirs
    partial = pl.pallas_call(
        expert_kernel,
        in_specs=in_vmem(1) + in_hbm(6),
        out_specs=pl.BlockSpec(memory_space=pltpu.VMEM),
        out_shape=jax.ShapeDtypeStruct((quarters, rows, share), jnp.bfloat16),
        scratch_shapes=[pltpu.VMEM(w.shape, w.dtype) for w in weights]
        + [pltpu.SemaphoreType.DMA((6,))],
        compiler_params=params,
        name="experts",
    )(x, *[far(w) for w in weights])
    partial = over("y", partial)
    summed = jnp.sum(partial.astype(jnp.float32), axis=0).astype(jnp.bfloat16)
    summed, *held = lax.optimization_barrier((summed, *held, *swapped))
    held, swapped = held[:quarters], held[quarters:]
    swapped.append(across(held[-1]))
    returned = over(WIDE, summed.reshape(experts, slots, share)).reshape(rows, share)
    mixed = pl.pallas_call(
        combine_kernel,
        in_specs=in_vmem(2),
        out_specs=pl.BlockSpec(memory_space=pltpu.VMEM),
        out_shape=jax.ShapeDtypeStruct((count, share), jnp.bfloat16),
        compiler_params=params,
        name="combine",
    )(table, returned)
    held = held + swapped
    near = (0, 1, 2)
    held = [held[i] if i in near else far(held[i]) for i in order_of(narrow, near)]
    parts = over(NARROW, mixed.reshape(narrow, own, share))

    half = own // 2
    residual, lo, hi, kernel = pl.pallas_call(
        lambda *refs: norm_kernel(quarters, cores, near, *refs),
        in_specs=in_hbm(1) + in_vmem(3) + in_hbm(5) + in_vmem(3),
        out_specs=in_vmem(4),
        out_shape=[
            jax.ShapeDtypeStruct((own, width), jnp.float32),
            jax.ShapeDtypeStruct((half, width), jnp.bfloat16),
            jax.ShapeDtypeStruct((half, width), jnp.bfloat16),
            jax.ShapeDtypeStruct((taps + 1, width), jnp.float32),
        ],
        scratch_shapes=[
            pltpu.VMEM((own, width), jnp.bfloat16),
            pltpu.VMEM((narrow - 3, packed_rows - width, channels), jnp.bfloat16),
            pltpu.SemaphoreType.DMA((narrow + 1,)),
        ],
        compiler_params=params,
        name="norm_glu",
    )(frames, *held, parts, norm_gain[None, :], norm_bias[None, :])

    ends = wide * narrow - 1
    left = lax.ppermute(hi, EVERY, [(i, i + 1) for i in range(ends)])
    right = lax.ppermute(lo, EVERY, [(i + 1, i) for i in range(ends)])
    return pl.pallas_call(
        lambda *refs: conv_kernel(quarters, cores, near, taps, *refs),
        in_specs=in_vmem(3) + in_hbm(5) + in_vmem(6),
        out_specs=pl.BlockSpec(memory_space=pltpu.VMEM),
        out_shape=jax.ShapeDtypeStruct((own, width), jnp.bfloat16),
        scratch_shapes=[
            pltpu.VMEM((own, width), jnp.bfloat16),
            pltpu.VMEM((narrow - 3, width, channels), jnp.bfloat16),
            pltpu.SemaphoreType.DMA((narrow,)),
        ],
        compiler_params=params,
        name="conv",
    )(*held, left, lo, hi, right, kernel, residual)


def solution(mesh):
    chips = Mesh(mesh.devices.reshape(4, 16, 4, 2), EVERY)
    return jax.shard_map(
        shards,
        mesh=chips,
        in_specs=(
            P(WIDE, None),
            P(WIDE, None),
            P(WIDE, None),
            P(WIDE, None, NARROW),
            P(WIDE, None, NARROW),
            P(WIDE, NARROW, None),
            P(),
            P(),
            P(None, None, NARROW),
            P(None, NARROW),
            P(NARROW, None),
        ),
        out_specs=P(EVERY, None),
        check_vma=False,
    )
```

```python
import jax
import jax.numpy as jnp
from jax import lax
from jax.experimental import pallas as pl
from jax.experimental.pallas import tpu as pltpu
from jax.sharding import Mesh
from jax.sharding import PartitionSpec as P

WIDE = ("x", "z")
NARROW = ("y", "c")
EVERY = ("x", "z", "y", "c")
VMEM_BYTES = 24 << 20


def in_vmem(count):
    return [pl.BlockSpec(memory_space=pltpu.VMEM)] * count


def mm(a, b):
    return jnp.dot(a, b, preferred_element_type=jnp.float32)


def fetched(copies):
    for copy in copies:
        copy.start()
    return copies


def prepare_kernel(
    experts,
    slots,
    ids_ref,
    frames_ref,
    in_ref,
    taps_ref,
    point_ref,
    gates_ref,
    out_ref,
    table_ref,
    packed_ref,
    held_ref,
    ids_vmem,
    gates_vmem,
    in_vmem_ref,
    taps_vmem,
    wide_ref,
    sem,
):
    both, lanes = in_ref.shape
    half = both // 2
    taps = taps_ref.shape[0]
    at = both + taps + 1
    count, share = held_ref.shape
    column = pl.multiple_of(lax.axis_index("y") * share, share)
    names, held, halves, kernel, gates, *points = fetched(
        [
            pltpu.make_async_copy(ids_ref, ids_vmem, sem.at[0]),
            pltpu.make_async_copy(frames_ref.at[:, pl.ds(column, share)], held_ref, sem.at[1]),
            pltpu.make_async_copy(in_ref, in_vmem_ref, sem.at[2]),
            pltpu.make_async_copy(taps_ref, taps_vmem, sem.at[3]),
            pltpu.make_async_copy(gates_ref, gates_vmem, sem.at[4]),
        ]
        + [
            pltpu.make_async_copy(
                point_ref.at[:, b * lanes : (b + 1) * lanes],
                packed_ref.at[at + b * lanes : at + (b + 1) * lanes, :],
                sem.at[5 + b],
            )
            for b in range(point_ref.shape[1] // lanes)
        ]
    )
    names.wait()
    ids = ids_vmem[...]
    first = lax.axis_index("c") * slots
    expert = lax.broadcasted_iota(jnp.int32, (experts, count), 0)
    named = [jnp.where(expert == ids[k : k + 1, :], 1.0, 0.0) for k in range(2)]
    before = lax.broadcasted_iota(jnp.int32, (count, count), 0) < lax.broadcasted_iota(
        jnp.int32, (count, count), 1
    )
    rank = mm(
        jnp.concatenate(named, axis=0).astype(jnp.bfloat16),
        jnp.where(before, 1.0, 0.0).astype(jnp.bfloat16),
    )
    total = jnp.sum(named[0], axis=1, keepdims=True)
    place = [
        jnp.sum(named[0] * rank[:experts], axis=0, keepdims=True),
        jnp.sum(named[1] * (rank[experts:] + total), axis=0, keepdims=True),
    ]
    row = lax.broadcasted_iota(jnp.int32, (experts * slots, count), 0)
    chosen = None
    targets = []
    for k in range(2):
        local = place[k].astype(jnp.int32) - first
        target = jnp.where(
            (local >= 0) & (local < slots), ids[k : k + 1, :] * slots + local, -1
        )
        targets.append(target.astype(jnp.float32))
        hit = row == target
        chosen = hit if chosen is None else chosen | hit
    pick = jnp.where(chosen, 1.0, 0.0).astype(jnp.bfloat16)
    held.wait()
    out_ref[...] = mm(pick, held_ref[...]).astype(jnp.bfloat16)
    halves.wait()
    wide_ref[...] = in_vmem_ref[...].astype(jnp.float32)
    packed_ref[:half, :] = wide_ref[pl.ds(0, half, 2), :].astype(jnp.bfloat16)
    packed_ref[half:both, :] = wide_ref[pl.ds(1, half, 2), :].astype(jnp.bfloat16)
    kernel.wait()
    packed_ref[both:at, :] = jnp.concatenate(
        [taps_vmem[...].astype(jnp.float32), jnp.zeros((1, lanes), jnp.float32)], axis=0
    ).astype(jnp.bfloat16)
    gates.wait()
    table_ref[...] = jnp.concatenate(
        targets + [gates_vmem[...], jnp.zeros((4, count), jnp.float32)], axis=0
    )
    for copy in points:
        copy.wait()


def expert_kernel(x_ref, *refs):
    sources, out_ref, held, sem = refs[:6], refs[6], refs[7:13], refs[13]
    copies = [pltpu.make_async_copy(s, h, sem.at[i]) for i, (s, h) in enumerate(zip(sources, held))]
    for i in (0, 1, 3, 4, 2, 5):
        copies[i].start()
    chunks, _, width = x_ref.shape
    x = jnp.concatenate([x_ref[q] for q in range(chunks)], axis=1)
    hidden = []
    for pair in range(2):
        copies[3 * pair].wait()
        gate = mm(x, held[3 * pair][...])
        copies[3 * pair + 1].wait()
        up = mm(x, held[3 * pair + 1][...])
        hidden.append((gate * jax.nn.sigmoid(gate) * up).astype(jnp.bfloat16))
    copies[2].wait()
    copies[5].wait()
    for q in range(chunks):
        cols = slice(q * width, (q + 1) * width)
        out_ref[q] = (mm(hidden[0], held[2][:, cols]) + mm(hidden[1], held[5][:, cols])).astype(
            jnp.bfloat16
        )


def blocks_of(quarters, cores, near):
    y, c = lax.axis_index("y"), lax.axis_index("c")
    index = [
        lax.rem(y + (2 * side - 1) * step + quarters, quarters) * cores + side
        for side in (c, cores - 1 - c)
        for step in range(quarters)
    ]
    return [index[i] for i in order_of(len(index), near)]


def order_of(count, near):
    return [i for i in range(count) if i in near] + [i for i in range(count) if i not in near]


def fetched_rows(near, first, last, refs, held_ref, sem):
    views = [(ref.at[first:last, :], None) for ref in refs[: len(near)]]
    for i, ref in enumerate(refs[len(near) :]):
        copy = pltpu.make_async_copy(ref.at[first:last, :], held_ref.at[i], sem.at[i])
        copy.start()
        views.append((held_ref.at[i], copy))
    return views


def combine_kernel(table_ref, rows_ref, out_ref):
    count = table_ref.shape[1]
    table = table_ref[...].T
    slot = lax.broadcasted_iota(jnp.int32, (count, rows_ref.shape[0]), 1)
    total = None
    for k in range(2):
        hit = slot == table[:, k : k + 1].astype(jnp.int32)
        picked = mm(jnp.where(hit, 1.0, 0.0).astype(jnp.bfloat16), rows_ref[...])
        picked = picked * table[:, 2 + k : 3 + k]
        total = picked if total is None else total + picked
    out_ref[...] = total.astype(jnp.bfloat16)


def norm_kernel(quarters, cores, near, frames_ref, *refs):
    count = quarters * cores
    parts_ref, gain_ref, bias_ref, res_ref, lo_ref, hi_ref, taps_ref, own_ref, held_ref, sem = refs[count:]
    own, width = own_ref.shape
    index = lax.axis_index("y") * cores + lax.axis_index("c")
    fetch = pltpu.make_async_copy(
        frames_ref.at[pl.ds(pl.multiple_of(index * own, own), own), :], own_ref, sem.at[count]
    )
    fetch.start()
    views = fetched_rows(near, 0, held_ref.shape[1], refs[:count], held_ref, sem)
    moe = jnp.concatenate(
        [
            parts_ref[2 * q].astype(jnp.float32) + parts_ref[2 * q + 1].astype(jnp.float32)
            for q in range(parts_ref.shape[0] // 2)
        ],
        axis=1,
    )
    fetch.wait()
    residual = own_ref[...].astype(jnp.float32) + moe
    res_ref[...] = residual
    centered = residual - jnp.mean(residual, axis=1, keepdims=True)
    variance = jnp.mean(centered * centered, axis=1, keepdims=True)
    normed = (centered / jnp.sqrt(variance + 1e-05) * gain_ref[...] + bias_ref[...]).astype(
        jnp.bfloat16
    )
    channels = width // count
    half, taps = lo_ref.shape[0], taps_ref.shape[0]
    for (ref, copy), index in zip(views, blocks_of(quarters, cores, near)):
        if copy is not None:
            copy.wait()
        both = jnp.concatenate([ref[:width, :], ref[width : 2 * width, :]], axis=1)
        projected = mm(normed, both)
        glu = projected[:, :channels] * jax.nn.sigmoid(projected[:, channels:])
        glu = glu.astype(jnp.bfloat16)
        cols = pl.ds(pl.multiple_of(index * channels, channels), channels)
        lo_ref[:, cols] = glu[:half]
        hi_ref[:, cols] = glu[half:]
        taps_ref[:, cols] = ref[2 * width : 2 * width + taps, :].astype(jnp.float32)


def conv_kernel(quarters, cores, near, taps, *refs):
    blocks = quarters * cores
    left_ref, lo_ref, hi_ref, right_ref, taps_ref, res_ref, out_ref, act_ref, held_ref, sem = refs[blocks:]
    half, width = lo_ref.shape
    count = 2 * half
    reach = (taps - 1) // 2
    channels = width // blocks
    first = 2 * width + taps + 1
    views = fetched_rows(near, first, first + width, refs[:blocks], held_ref, sem)
    for n in range(0, blocks, 2):
        cols = slice(n * channels, (n + 2) * channels)
        window = jnp.concatenate(
            [ref[:, cols] for ref in (left_ref, lo_ref, hi_ref, right_ref)], axis=0
        ).astype(jnp.float32)
        depth = None
        for turn in range(8):
            moved = pltpu.roll(window, 2 * count - turn, 0) if turn else window
            for j in range(taps):
                start = half - reach + j
                if start % 8 == turn:
                    term = moved[start - turn : start - turn + count] * taps_ref[j : j + 1, cols]
                    depth = term if depth is None else depth + term
        act_ref[:, cols] = (depth * jax.nn.sigmoid(depth)).astype(jnp.bfloat16)
    acts, points = [], []
    for (ref, copy), index in zip(views, blocks_of(quarters, cores, near)):
        if copy is not None:
            copy.wait()
        acts.append(act_ref[:, pl.ds(pl.multiple_of(index * channels, channels), channels)])
        points.append(
            jnp.concatenate(
                [ref[b * channels : (b + 1) * channels, :] for b in range(blocks)],
                axis=1,
            )
        )
    total = res_ref[...] + mm(jnp.concatenate(acts, axis=1), jnp.concatenate(points, axis=0))
    out_ref[...] = total.astype(jnp.bfloat16)


def shards(
    frames,
    expert_ids,
    gate_values,
    w_gate,
    w_up,
    w_down,
    norm_gain,
    norm_bias,
    point_in,
    depth_kernel,
    point_out,
):
    count, width = frames.shape
    wide = lax.axis_size("x") * lax.axis_size("z")
    quarters, cores = lax.axis_size("y"), lax.axis_size("c")
    narrow = quarters * cores
    experts = w_gate.shape[0] * wide
    slots = 2 * expert_ids.shape[1] * count // experts // cores
    share = width // quarters
    own = count // narrow
    taps, channels = depth_kernel.shape
    params = pltpu.CompilerParams(vmem_limit_bytes=VMEM_BYTES)

    in_hbm = lambda n: [pl.BlockSpec(memory_space=pltpu.HBM)] * n
    far = lambda array: pltpu.with_memory_space_constraint(array, pltpu.HBM)
    frames = far(frames)

    rows = experts * slots
    packed_rows = 3 * width + taps + 1
    outgoing, table, packed = pl.pallas_call(
        lambda *refs: prepare_kernel(experts, slots, *refs),
        in_specs=in_hbm(6),
        out_specs=in_vmem(3),
        out_shape=[
            jax.ShapeDtypeStruct((rows, share), jnp.bfloat16),
            jax.ShapeDtypeStruct((8, count), jnp.float32),
            jax.ShapeDtypeStruct((packed_rows, channels), jnp.bfloat16),
        ],
        scratch_shapes=[
            pltpu.VMEM((count, share), jnp.bfloat16),
            pltpu.VMEM((2, count), jnp.int32),
            pltpu.VMEM((2, count), jnp.float32),
            pltpu.VMEM((2 * width, channels), jnp.bfloat16),
            pltpu.VMEM((taps, channels), jnp.bfloat16),
            pltpu.VMEM((2 * width, channels), jnp.float32),
            pltpu.SemaphoreType.DMA((5 + narrow,)),
        ],
        compiler_params=params,
        name="prepare",
    )(
        far(expert_ids.T),
        frames,
        far(point_in.reshape(2 * width, channels)),
        far(depth_kernel),
        far(point_out),
        far(gate_values.T),
    )

    ring = [
        (y * cores + c, (y + 1 - 2 * c) % quarters * cores + c)
        for y in range(quarters)
        for c in range(cores)
    ]
    swap = [(i, cores - 1 - i) for i in range(cores)]
    around = lambda cells: lax.ppermute(cells, NARROW, ring)
    across = lambda cells: lax.ppermute(cells, "c", swap)
    held = [packed, around(packed)]

    def over(axis, cells):
        return lax.all_to_all(cells, axis, split_axis=0, concat_axis=0, tiled=True)

    arrived = over(WIDE, outgoing.reshape(experts, slots, share)).reshape(1, rows, share)
    mine = [w_gate[0], w_up[0], w_down[0]]
    theirs = [across(w) for w in mine]
    arrived, *held = lax.optimization_barrier((arrived, *held))
    swapped = [across(cells) for cells in held]
    held.append(around(held[-1]))
    x = over("y", jnp.broadcast_to(arrived, (quarters, rows, share)))
    weights = mine + theirs
    partial = pl.pallas_call(
        expert_kernel,
        in_specs=in_vmem(1) + in_hbm(6),
        out_specs=pl.BlockSpec(memory_space=pltpu.VMEM),
        out_shape=jax.ShapeDtypeStruct((quarters, rows, share), jnp.bfloat16),
        scratch_shapes=[pltpu.VMEM(w.shape, w.dtype) for w in weights]
        + [pltpu.SemaphoreType.DMA((6,))],
        compiler_params=params,
        name="experts",
    )(x, *[far(w) for w in weights])
    partial = over("y", partial)
    summed = jnp.sum(partial.astype(jnp.float32), axis=0).astype(jnp.bfloat16)
    summed, *held = lax.optimization_barrier((summed, *held, *swapped))
    held, swapped = held[: quarters - 1], held[quarters - 1 :]
    swapped.append(across(held[-1]))
    back = [(b, a) for a, b in ring]
    held.append(lax.ppermute(held[0], NARROW, back))
    swapped.append(lax.ppermute(held[0], NARROW, [(a, b ^ 1) for a, b in back]))
    returned = over(WIDE, summed.reshape(experts, slots, share)).reshape(rows, share)
    mixed = pl.pallas_call(
        combine_kernel,
        in_specs=in_vmem(2),
        out_specs=pl.BlockSpec(memory_space=pltpu.VMEM),
        out_shape=jax.ShapeDtypeStruct((count, share), jnp.bfloat16),
        compiler_params=params,
        name="combine",
    )(table, returned)
    held = held + swapped
    near = (0, 1, 2)
    held = [held[i] if i in near else far(held[i]) for i in order_of(narrow, near)]
    parts = over(NARROW, mixed.reshape(narrow, own, share))

    half = own // 2
    residual, lo, hi, kernel = pl.pallas_call(
        lambda *refs: norm_kernel(quarters, cores, near, *refs),
        in_specs=in_hbm(1) + in_vmem(3) + in_hbm(5) + in_vmem(3),
        out_specs=in_vmem(4),
        out_shape=[
            jax.ShapeDtypeStruct((own, width), jnp.float32),
            jax.ShapeDtypeStruct((half, width), jnp.bfloat16),
            jax.ShapeDtypeStruct((half, width), jnp.bfloat16),
            jax.ShapeDtypeStruct((taps + 1, width), jnp.float32),
        ],
        scratch_shapes=[
            pltpu.VMEM((own, width), jnp.bfloat16),
            pltpu.VMEM((narrow - 3, packed_rows - width, channels), jnp.bfloat16),
            pltpu.SemaphoreType.DMA((narrow + 1,)),
        ],
        compiler_params=params,
        name="norm_glu",
    )(frames, *held, parts, norm_gain[None, :], norm_bias[None, :])

    ends = wide * narrow - 1
    left = lax.ppermute(hi, EVERY, [(i, i + 1) for i in range(ends)])
    right = lax.ppermute(lo, EVERY, [(i + 1, i) for i in range(ends)])
    return pl.pallas_call(
        lambda *refs: conv_kernel(quarters, cores, near, taps, *refs),
        in_specs=in_vmem(3) + in_hbm(5) + in_vmem(6),
        out_specs=pl.BlockSpec(memory_space=pltpu.VMEM),
        out_shape=jax.ShapeDtypeStruct((own, width), jnp.bfloat16),
        scratch_shapes=[
            pltpu.VMEM((own, width), jnp.bfloat16),
            pltpu.VMEM((narrow - 3, width, channels), jnp.bfloat16),
            pltpu.SemaphoreType.DMA((narrow,)),
        ],
        compiler_params=params,
        name="conv",
    )(*held, left, lo, hi, right, kernel, residual)


def solution(mesh):
    chips = Mesh(mesh.devices.reshape(4, 16, 4, 2), EVERY)
    return jax.shard_map(
        shards,
        mesh=chips,
        in_specs=(
            P(WIDE, None),
            P(WIDE, None),
            P(WIDE, None),
            P(WIDE, None, NARROW),
            P(WIDE, None, NARROW),
            P(WIDE, NARROW, None),
            P(),
            P(),
            P(None, None, NARROW),
            P(None, NARROW),
            P(NARROW, None),
        ),
        out_specs=P(EVERY, None),
        check_vma=False,
    )
```

```python
import jax
import jax.numpy as jnp
from jax import lax
from jax.experimental import pallas as pl
from jax.experimental.pallas import tpu as pltpu
from jax.sharding import Mesh
from jax.sharding import PartitionSpec as P

WIDE = ("x", "z")
NARROW = ("y", "c")
EVERY = ("x", "z", "y", "c")
VMEM_BYTES = 24 << 20


def in_vmem(count):
    return [pl.BlockSpec(memory_space=pltpu.VMEM)] * count


def mm(a, b):
    return jnp.dot(a, b, preferred_element_type=jnp.float32)


def fetched(copies):
    for copy in copies:
        copy.start()
    return copies


def prepare_kernel(
    experts,
    slots,
    ids_ref,
    frames_ref,
    in_ref,
    taps_ref,
    point_ref,
    gates_ref,
    out_ref,
    table_ref,
    packed_ref,
    held_ref,
    ids_vmem,
    gates_vmem,
    in_vmem_ref,
    taps_vmem,
    wide_ref,
    sem,
):
    both, lanes = in_ref.shape
    half = both // 2
    taps = taps_ref.shape[0]
    at = both + taps + 1
    count, share = held_ref.shape
    column = pl.multiple_of(lax.axis_index("y") * share, share)
    names, held, halves, kernel, gates, *points = fetched(
        [
            pltpu.make_async_copy(ids_ref, ids_vmem, sem.at[0]),
            pltpu.make_async_copy(frames_ref.at[:, pl.ds(column, share)], held_ref, sem.at[1]),
            pltpu.make_async_copy(in_ref, in_vmem_ref, sem.at[2]),
            pltpu.make_async_copy(taps_ref, taps_vmem, sem.at[3]),
            pltpu.make_async_copy(gates_ref, gates_vmem, sem.at[4]),
        ]
        + [
            pltpu.make_async_copy(
                point_ref.at[:, b * lanes : (b + 1) * lanes],
                packed_ref.at[at + b * lanes : at + (b + 1) * lanes, :],
                sem.at[5 + b],
            )
            for b in range(point_ref.shape[1] // lanes)
        ]
    )
    names.wait()
    ids = ids_vmem[...]
    first = lax.axis_index("c") * slots
    expert = lax.broadcasted_iota(jnp.int32, (experts, count), 0)
    named = [jnp.where(expert == ids[k : k + 1, :], 1.0, 0.0) for k in range(2)]
    before = lax.broadcasted_iota(jnp.int32, (count, count), 0) < lax.broadcasted_iota(
        jnp.int32, (count, count), 1
    )
    rank = mm(
        jnp.concatenate(named, axis=0).astype(jnp.bfloat16),
        jnp.where(before, 1.0, 0.0).astype(jnp.bfloat16),
    )
    total = jnp.sum(named[0], axis=1, keepdims=True)
    place = [
        jnp.sum(named[0] * rank[:experts], axis=0, keepdims=True),
        jnp.sum(named[1] * (rank[experts:] + total), axis=0, keepdims=True),
    ]
    row = lax.broadcasted_iota(jnp.int32, (experts * slots, count), 0)
    chosen = None
    targets = []
    for k in range(2):
        local = place[k].astype(jnp.int32) - first
        target = jnp.where(
            (local >= 0) & (local < slots), ids[k : k + 1, :] * slots + local, -1
        )
        targets.append(target.astype(jnp.float32))
        hit = row == target
        chosen = hit if chosen is None else chosen | hit
    pick = jnp.where(chosen, 1.0, 0.0).astype(jnp.bfloat16)
    held.wait()
    out_ref[...] = mm(pick, held_ref[...]).astype(jnp.bfloat16)
    halves.wait()
    wide_ref[...] = in_vmem_ref[...].astype(jnp.float32)
    packed_ref[:half, :] = wide_ref[pl.ds(0, half, 2), :].astype(jnp.bfloat16)
    packed_ref[half:both, :] = wide_ref[pl.ds(1, half, 2), :].astype(jnp.bfloat16)
    kernel.wait()
    packed_ref[both:at, :] = jnp.concatenate(
        [taps_vmem[...].astype(jnp.float32), jnp.zeros((1, lanes), jnp.float32)], axis=0
    ).astype(jnp.bfloat16)
    gates.wait()
    table_ref[...] = jnp.concatenate(
        targets + [gates_vmem[...], jnp.zeros((4, count), jnp.float32)], axis=0
    )
    for copy in points:
        copy.wait()


def expert_kernel(x_ref, *refs):
    sources, out_ref, held, sem = refs[:6], refs[6], refs[7:13], refs[13]
    copies = [pltpu.make_async_copy(s, h, sem.at[i]) for i, (s, h) in enumerate(zip(sources, held))]
    for i in (0, 1, 3, 4, 2, 5):
        copies[i].start()
    chunks, _, width = x_ref.shape
    x = jnp.concatenate([x_ref[q] for q in range(chunks)], axis=1)
    hidden = []
    for pair in range(2):
        copies[3 * pair].wait()
        gate = mm(x, held[3 * pair][...])
        copies[3 * pair + 1].wait()
        up = mm(x, held[3 * pair + 1][...])
        hidden.append((gate * jax.nn.sigmoid(gate) * up).astype(jnp.bfloat16))
    copies[2].wait()
    copies[5].wait()
    for q in range(chunks):
        cols = slice(q * width, (q + 1) * width)
        out_ref[q] = (mm(hidden[0], held[2][:, cols]) + mm(hidden[1], held[5][:, cols])).astype(
            jnp.bfloat16
        )


def blocks_of(quarters, cores, near):
    y, c = lax.axis_index("y"), lax.axis_index("c")
    index = [
        lax.rem(y + (1 - 2 * side) * step + quarters, quarters) * cores + side
        for side in (c, cores - 1 - c)
        for step in range(quarters)
    ]
    return [index[i] for i in order_of(len(index), near)]


def order_of(count, near):
    return [i for i in range(count) if i in near] + [i for i in range(count) if i not in near]


def fetched_rows(near, first, last, refs, held_ref, sem):
    views = [(ref.at[first:last, :], None) for ref in refs[: len(near)]]
    for i, ref in enumerate(refs[len(near) :]):
        copy = pltpu.make_async_copy(ref.at[first:last, :], held_ref.at[i], sem.at[i])
        copy.start()
        views.append((held_ref.at[i], copy))
    return views


def combine_kernel(table_ref, rows_ref, out_ref):
    count = table_ref.shape[1]
    table = table_ref[...].T
    slot = lax.broadcasted_iota(jnp.int32, (count, rows_ref.shape[0]), 1)
    total = None
    for k in range(2):
        hit = slot == table[:, k : k + 1].astype(jnp.int32)
        picked = mm(jnp.where(hit, 1.0, 0.0).astype(jnp.bfloat16), rows_ref[...])
        picked = picked * table[:, 2 + k : 3 + k]
        total = picked if total is None else total + picked
    out_ref[...] = total.astype(jnp.bfloat16)


def norm_kernel(quarters, cores, near, frames_ref, *refs):
    count = quarters * cores
    parts_ref, gain_ref, bias_ref, res_ref, lo_ref, hi_ref, taps_ref, own_ref, held_ref, sem = refs[count:]
    own, width = own_ref.shape
    index = lax.axis_index("y") * cores + lax.axis_index("c")
    fetch = pltpu.make_async_copy(
        frames_ref.at[pl.ds(pl.multiple_of(index * own, own), own), :], own_ref, sem.at[count]
    )
    fetch.start()
    views = fetched_rows(near, 0, held_ref.shape[1], refs[:count], held_ref, sem)
    moe = jnp.concatenate(
        [
            parts_ref[2 * q].astype(jnp.float32) + parts_ref[2 * q + 1].astype(jnp.float32)
            for q in range(parts_ref.shape[0] // 2)
        ],
        axis=1,
    )
    fetch.wait()
    residual = own_ref[...].astype(jnp.float32) + moe
    res_ref[...] = residual
    centered = residual - jnp.mean(residual, axis=1, keepdims=True)
    variance = jnp.mean(centered * centered, axis=1, keepdims=True)
    normed = (centered / jnp.sqrt(variance + 1e-05) * gain_ref[...] + bias_ref[...]).astype(
        jnp.bfloat16
    )
    channels = width // count
    half, taps = lo_ref.shape[0], taps_ref.shape[0]
    for (ref, copy), index in zip(views, blocks_of(quarters, cores, near)):
        if copy is not None:
            copy.wait()
        both = jnp.concatenate([ref[:width, :], ref[width : 2 * width, :]], axis=1)
        projected = mm(normed, both)
        glu = projected[:, :channels] * jax.nn.sigmoid(projected[:, channels:])
        glu = glu.astype(jnp.bfloat16)
        cols = pl.ds(pl.multiple_of(index * channels, channels), channels)
        lo_ref[:, cols] = glu[:half]
        hi_ref[:, cols] = glu[half:]
        taps_ref[:, cols] = ref[2 * width : 2 * width + taps, :].astype(jnp.float32)


def conv_kernel(quarters, cores, near, taps, *refs):
    blocks = quarters * cores
    left_ref, lo_ref, hi_ref, right_ref, taps_ref, res_ref, out_ref, act_ref, held_ref, sem = refs[blocks:]
    half, width = lo_ref.shape
    count = 2 * half
    reach = (taps - 1) // 2
    channels = width // blocks
    first = 2 * width + taps + 1
    views = fetched_rows(near, first, first + width, refs[:blocks], held_ref, sem)
    for n in range(0, blocks, 2):
        cols = slice(n * channels, (n + 2) * channels)
        window = jnp.concatenate(
            [ref[:, cols] for ref in (left_ref, lo_ref, hi_ref, right_ref)], axis=0
        ).astype(jnp.float32)
        depth = None
        for turn in range(8):
            moved = pltpu.roll(window, 2 * count - turn, 0) if turn else window
            for j in range(taps):
                start = half - reach + j
                if start % 8 == turn:
                    term = moved[start - turn : start - turn + count] * taps_ref[j : j + 1, cols]
                    depth = term if depth is None else depth + term
        act_ref[:, cols] = (depth * jax.nn.sigmoid(depth)).astype(jnp.bfloat16)
    acts, points = [], []
    for (ref, copy), index in zip(views, blocks_of(quarters, cores, near)):
        if copy is not None:
            copy.wait()
        acts.append(act_ref[:, pl.ds(pl.multiple_of(index * channels, channels), channels)])
        points.append(
            jnp.concatenate(
                [ref[b * channels : (b + 1) * channels, :] for b in range(blocks)],
                axis=1,
            )
        )
    total = res_ref[...] + mm(jnp.concatenate(acts, axis=1), jnp.concatenate(points, axis=0))
    out_ref[...] = total.astype(jnp.bfloat16)


def shards(
    frames,
    expert_ids,
    gate_values,
    w_gate,
    w_up,
    w_down,
    norm_gain,
    norm_bias,
    point_in,
    depth_kernel,
    point_out,
):
    count, width = frames.shape
    wide = lax.axis_size("x") * lax.axis_size("z")
    quarters, cores = lax.axis_size("y"), lax.axis_size("c")
    narrow = quarters * cores
    experts = w_gate.shape[0] * wide
    slots = 2 * expert_ids.shape[1] * count // experts // cores
    share = width // quarters
    own = count // narrow
    taps, channels = depth_kernel.shape
    params = pltpu.CompilerParams(vmem_limit_bytes=VMEM_BYTES)

    in_hbm = lambda n: [pl.BlockSpec(memory_space=pltpu.HBM)] * n
    far = lambda array: pltpu.with_memory_space_constraint(array, pltpu.HBM)
    frames = far(frames)

    rows = experts * slots
    packed_rows = 3 * width + taps + 1
    outgoing, table, packed = pl.pallas_call(
        lambda *refs: prepare_kernel(experts, slots, *refs),
        in_specs=in_hbm(6),
        out_specs=in_vmem(3),
        out_shape=[
            jax.ShapeDtypeStruct((rows, share), jnp.bfloat16),
            jax.ShapeDtypeStruct((8, count), jnp.float32),
            jax.ShapeDtypeStruct((packed_rows, channels), jnp.bfloat16),
        ],
        scratch_shapes=[
            pltpu.VMEM((count, share), jnp.bfloat16),
            pltpu.VMEM((2, count), jnp.int32),
            pltpu.VMEM((2, count), jnp.float32),
            pltpu.VMEM((2 * width, channels), jnp.bfloat16),
            pltpu.VMEM((taps, channels), jnp.bfloat16),
            pltpu.VMEM((2 * width, channels), jnp.float32),
            pltpu.SemaphoreType.DMA((5 + narrow,)),
        ],
        compiler_params=params,
        name="prepare",
    )(
        far(expert_ids.T),
        frames,
        far(point_in.reshape(2 * width, channels)),
        far(depth_kernel),
        far(point_out),
        far(gate_values.T),
    )

    ring = [
        (y * cores + c, (y - 1 + 2 * c) % quarters * cores + c)
        for y in range(quarters)
        for c in range(cores)
    ]
    swap = [(i, cores - 1 - i) for i in range(cores)]
    around = lambda cells: lax.ppermute(cells, NARROW, ring)
    across = lambda cells: lax.ppermute(cells, "c", swap)
    held = [packed, around(packed)]

    def over(axis, cells):
        return lax.all_to_all(cells, axis, split_axis=0, concat_axis=0, tiled=True)

    arrived = over(WIDE, outgoing.reshape(experts, slots, share)).reshape(1, rows, share)
    mine = [w_gate[0], w_up[0], w_down[0]]
    theirs = [across(w) for w in mine]
    arrived, *held = lax.optimization_barrier((arrived, *held))
    swapped = [across(cells) for cells in held]
    held.append(around(held[-1]))
    x = over("y", jnp.broadcast_to(arrived, (quarters, rows, share)))
    weights = mine + theirs
    partial = pl.pallas_call(
        expert_kernel,
        in_specs=in_vmem(1) + in_hbm(6),
        out_specs=pl.BlockSpec(memory_space=pltpu.VMEM),
        out_shape=jax.ShapeDtypeStruct((quarters, rows, share), jnp.bfloat16),
        scratch_shapes=[pltpu.VMEM(w.shape, w.dtype) for w in weights]
        + [pltpu.SemaphoreType.DMA((6,))],
        compiler_params=params,
        name="experts",
    )(x, *[far(w) for w in weights])
    partial = over("y", partial)
    summed = jnp.sum(partial.astype(jnp.float32), axis=0).astype(jnp.bfloat16)
    summed, *held = lax.optimization_barrier((summed, *held, *swapped))
    held, swapped = held[: quarters - 1], held[quarters - 1 :]
    swapped.append(across(held[-1]))
    back = [(b, a) for a, b in ring]
    held.append(lax.ppermute(held[0], NARROW, back))
    swapped.append(lax.ppermute(held[0], NARROW, [(a, b ^ 1) for a, b in back]))
    returned = over(WIDE, summed.reshape(experts, slots, share)).reshape(rows, share)
    mixed = pl.pallas_call(
        combine_kernel,
        in_specs=in_vmem(2),
        out_specs=pl.BlockSpec(memory_space=pltpu.VMEM),
        out_shape=jax.ShapeDtypeStruct((count, share), jnp.bfloat16),
        compiler_params=params,
        name="combine",
    )(table, returned)
    held = held + swapped
    near = (0, 1, 2)
    held = [held[i] if i in near else far(held[i]) for i in order_of(narrow, near)]
    parts = over(NARROW, mixed.reshape(narrow, own, share))

    half = own // 2
    residual, lo, hi, kernel = pl.pallas_call(
        lambda *refs: norm_kernel(quarters, cores, near, *refs),
        in_specs=in_hbm(1) + in_vmem(3) + in_hbm(5) + in_vmem(3),
        out_specs=in_vmem(4),
        out_shape=[
            jax.ShapeDtypeStruct((own, width), jnp.float32),
            jax.ShapeDtypeStruct((half, width), jnp.bfloat16),
            jax.ShapeDtypeStruct((half, width), jnp.bfloat16),
            jax.ShapeDtypeStruct((taps + 1, width), jnp.float32),
        ],
        scratch_shapes=[
            pltpu.VMEM((own, width), jnp.bfloat16),
            pltpu.VMEM((narrow - 3, packed_rows - width, channels), jnp.bfloat16),
            pltpu.SemaphoreType.DMA((narrow + 1,)),
        ],
        compiler_params=params,
        name="norm_glu",
    )(frames, *held, parts, norm_gain[None, :], norm_bias[None, :])

    ends = wide * narrow - 1
    left = lax.ppermute(hi, EVERY, [(i, i + 1) for i in range(ends)])
    right = lax.ppermute(lo, EVERY, [(i + 1, i) for i in range(ends)])
    return pl.pallas_call(
        lambda *refs: conv_kernel(quarters, cores, near, taps, *refs),
        in_specs=in_vmem(3) + in_hbm(5) + in_vmem(6),
        out_specs=pl.BlockSpec(memory_space=pltpu.VMEM),
        out_shape=jax.ShapeDtypeStruct((own, width), jnp.bfloat16),
        scratch_shapes=[
            pltpu.VMEM((own, width), jnp.bfloat16),
            pltpu.VMEM((narrow - 3, width, channels), jnp.bfloat16),
            pltpu.SemaphoreType.DMA((narrow,)),
        ],
        compiler_params=params,
        name="conv",
    )(*held, left, lo, hi, right, kernel, residual)


def solution(mesh):
    chips = Mesh(mesh.devices.reshape(4, 16, 4, 2), EVERY)
    return jax.shard_map(
        shards,
        mesh=chips,
        in_specs=(
            P(WIDE, None),
            P(WIDE, None),
            P(WIDE, None),
            P(WIDE, None, NARROW),
            P(WIDE, None, NARROW),
            P(WIDE, NARROW, None),
            P(),
            P(),
            P(None, None, NARROW),
            P(None, NARROW),
            P(NARROW, None),
        ),
        out_specs=P(EVERY, None),
        check_vma=False,
    )
```

```python
import jax
import jax.numpy as jnp
from jax import lax
from jax.experimental import pallas as pl
from jax.experimental.pallas import tpu as pltpu
from jax.sharding import Mesh
from jax.sharding import PartitionSpec as P

WIDE = ("x", "z")
NARROW = ("y", "c")
EVERY = ("x", "z", "y", "c")
VMEM_BYTES = 24 << 20


def in_vmem(count):
    return [pl.BlockSpec(memory_space=pltpu.VMEM)] * count


def mm(a, b):
    return jnp.dot(a, b, preferred_element_type=jnp.float32)


def fetched(copies):
    for copy in copies:
        copy.start()
    return copies


def prepare_kernel(
    experts,
    slots,
    ids_ref,
    frames_ref,
    in_ref,
    taps_ref,
    point_ref,
    gates_ref,
    out_ref,
    table_ref,
    packed_ref,
    held_ref,
    ids_vmem,
    gates_vmem,
    in_vmem_ref,
    taps_vmem,
    wide_ref,
    sem,
):
    both, lanes = in_ref.shape
    half = both // 2
    taps = taps_ref.shape[0]
    at = both + taps + 1
    count, share = held_ref.shape
    column = pl.multiple_of(lax.axis_index("y") * share, share)
    names, held, halves, kernel, gates, *points = fetched(
        [
            pltpu.make_async_copy(ids_ref, ids_vmem, sem.at[0]),
            pltpu.make_async_copy(frames_ref.at[:, pl.ds(column, share)], held_ref, sem.at[1]),
            pltpu.make_async_copy(in_ref, in_vmem_ref, sem.at[2]),
            pltpu.make_async_copy(taps_ref, taps_vmem, sem.at[3]),
            pltpu.make_async_copy(gates_ref, gates_vmem, sem.at[4]),
        ]
        + [
            pltpu.make_async_copy(
                point_ref.at[:, b * lanes : (b + 1) * lanes],
                packed_ref.at[at + b * lanes : at + (b + 1) * lanes, :],
                sem.at[5 + b],
            )
            for b in range(point_ref.shape[1] // lanes)
        ]
    )
    names.wait()
    ids = ids_vmem[...]
    first = lax.axis_index("c") * slots
    expert = lax.broadcasted_iota(jnp.int32, (experts, count), 0)
    named = [jnp.where(expert == ids[k : k + 1, :], 1.0, 0.0) for k in range(2)]
    before = lax.broadcasted_iota(jnp.int32, (count, count), 0) < lax.broadcasted_iota(
        jnp.int32, (count, count), 1
    )
    rank = mm(
        jnp.concatenate(named, axis=0).astype(jnp.bfloat16),
        jnp.where(before, 1.0, 0.0).astype(jnp.bfloat16),
    )
    total = jnp.sum(named[0], axis=1, keepdims=True)
    place = [
        jnp.sum(named[0] * rank[:experts], axis=0, keepdims=True),
        jnp.sum(named[1] * (rank[experts:] + total), axis=0, keepdims=True),
    ]
    row = lax.broadcasted_iota(jnp.int32, (experts * slots, count), 0)
    chosen = None
    targets = []
    for k in range(2):
        local = place[k].astype(jnp.int32) - first
        target = jnp.where(
            (local >= 0) & (local < slots), ids[k : k + 1, :] * slots + local, -1
        )
        targets.append(target.astype(jnp.float32))
        hit = row == target
        chosen = hit if chosen is None else chosen | hit
    pick = jnp.where(chosen, 1.0, 0.0).astype(jnp.bfloat16)
    held.wait()
    out_ref[...] = mm(pick, held_ref[...]).astype(jnp.bfloat16)
    halves.wait()
    wide_ref[...] = in_vmem_ref[...].astype(jnp.float32)
    packed_ref[:half, :] = wide_ref[pl.ds(0, half, 2), :].astype(jnp.bfloat16)
    packed_ref[half:both, :] = wide_ref[pl.ds(1, half, 2), :].astype(jnp.bfloat16)
    kernel.wait()
    packed_ref[both:at, :] = jnp.concatenate(
        [taps_vmem[...].astype(jnp.float32), jnp.zeros((1, lanes), jnp.float32)], axis=0
    ).astype(jnp.bfloat16)
    gates.wait()
    table_ref[...] = jnp.concatenate(
        targets + [gates_vmem[...], jnp.zeros((4, count), jnp.float32)], axis=0
    )
    for copy in points:
        copy.wait()


def repeat_kernel(cells_ref, out_ref, sem):
    for copy in fetched(
        [
            pltpu.make_async_copy(cells_ref, out_ref.at[q], sem.at[q])
            for q in range(out_ref.shape[0])
        ]
    ):
        copy.wait()


def sum_kernel(parts_ref, out_ref):
    total = parts_ref[0].astype(jnp.float32)
    for q in range(1, parts_ref.shape[0]):
        total = total + parts_ref[q].astype(jnp.float32)
    out_ref[...] = total.astype(jnp.bfloat16)


def expert_kernel(x_ref, *refs):
    sources, out_ref, held, sem = refs[:6], refs[6], refs[7:13], refs[13]
    copies = [pltpu.make_async_copy(s, h, sem.at[i]) for i, (s, h) in enumerate(zip(sources, held))]
    for i in (0, 1, 3, 4, 2, 5):
        copies[i].start()
    chunks, _, width = x_ref.shape
    x = jnp.concatenate([x_ref[q] for q in range(chunks)], axis=1)
    hidden = []
    for pair in range(2):
        copies[3 * pair].wait()
        gate = mm(x, held[3 * pair][...])
        copies[3 * pair + 1].wait()
        up = mm(x, held[3 * pair + 1][...])
        hidden.append((gate * jax.nn.sigmoid(gate) * up).astype(jnp.bfloat16))
    copies[2].wait()
    copies[5].wait()
    for q in range(chunks):
        cols = slice(q * width, (q + 1) * width)
        out_ref[q] = (mm(hidden[0], held[2][:, cols]) + mm(hidden[1], held[5][:, cols])).astype(
            jnp.bfloat16
        )


def blocks_of(quarters, cores, near):
    y, c = lax.axis_index("y"), lax.axis_index("c")
    index = [
        lax.rem(y + (1 - 2 * side) * step + quarters, quarters) * cores + side
        for side in (c, cores - 1 - c)
        for step in range(quarters)
    ]
    return [index[i] for i in order_of(len(index), near)]


def order_of(count, near):
    return [i for i in range(count) if i in near] + [i for i in range(count)[::-1] if i not in near]


def fetched_rows(near, first, last, refs, held_ref, sem):
    views = [(ref.at[first:last, :], None) for ref in refs[: len(near)]]
    for i, ref in enumerate(refs[len(near) :]):
        copy = pltpu.make_async_copy(ref.at[first:last, :], held_ref.at[i], sem.at[i])
        copy.start()
        views.append((held_ref.at[i], copy))
    return views


def combine_kernel(table_ref, rows_ref, out_ref):
    count = table_ref.shape[1]
    table = table_ref[...].T
    slot = lax.broadcasted_iota(jnp.int32, (count, rows_ref.shape[0]), 1)
    total = None
    for k in range(2):
        hit = slot == table[:, k : k + 1].astype(jnp.int32)
        picked = mm(jnp.where(hit, 1.0, 0.0).astype(jnp.bfloat16), rows_ref[...])
        picked = picked * table[:, 2 + k : 3 + k]
        total = picked if total is None else total + picked
    out_ref[...] = total.astype(jnp.bfloat16)


def norm_kernel(quarters, cores, near, frames_ref, *refs):
    count = quarters * cores
    parts_ref, gain_ref, bias_ref, res_ref, lo_ref, hi_ref, taps_ref, own_ref, held_ref, sem = refs[count:]
    own, width = own_ref.shape
    index = lax.axis_index("y") * cores + lax.axis_index("c")
    fetch = pltpu.make_async_copy(
        frames_ref.at[pl.ds(pl.multiple_of(index * own, own), own), :], own_ref, sem.at[count]
    )
    fetch.start()
    views = fetched_rows(near, 0, held_ref.shape[1], refs[:count], held_ref, sem)
    moe = jnp.concatenate(
        [
            parts_ref[2 * q].astype(jnp.float32) + parts_ref[2 * q + 1].astype(jnp.float32)
            for q in range(parts_ref.shape[0] // 2)
        ],
        axis=1,
    )
    fetch.wait()
    residual = own_ref[...].astype(jnp.float32) + moe
    res_ref[...] = residual
    centered = residual - jnp.mean(residual, axis=1, keepdims=True)
    variance = jnp.mean(centered * centered, axis=1, keepdims=True)
    normed = (centered / jnp.sqrt(variance + 1e-05) * gain_ref[...] + bias_ref[...]).astype(
        jnp.bfloat16
    )
    channels = width // count
    half, taps = lo_ref.shape[0], taps_ref.shape[0]
    for (ref, copy), index in zip(views, blocks_of(quarters, cores, near)):
        if copy is not None:
            copy.wait()
        both = jnp.concatenate([ref[:width, :], ref[width : 2 * width, :]], axis=1)
        projected = mm(normed, both)
        glu = projected[:, :channels] * jax.nn.sigmoid(projected[:, channels:])
        glu = glu.astype(jnp.bfloat16)
        cols = pl.ds(pl.multiple_of(index * channels, channels), channels)
        lo_ref[:, cols] = glu[:half]
        hi_ref[:, cols] = glu[half:]
        taps_ref[:, cols] = ref[2 * width : 2 * width + taps, :].astype(jnp.float32)


def conv_kernel(quarters, cores, near, taps, *refs):
    blocks = quarters * cores
    left_ref, lo_ref, hi_ref, right_ref, taps_ref, res_ref, out_ref, act_ref, held_ref, sem = refs[blocks:]
    half, width = lo_ref.shape
    count = 2 * half
    reach = (taps - 1) // 2
    channels = width // blocks
    first = 2 * width + taps + 1
    views = fetched_rows(near, first, first + width, refs[:blocks], held_ref, sem)
    for n in range(0, blocks, 2):
        cols = slice(n * channels, (n + 2) * channels)
        window = jnp.concatenate(
            [ref[:, cols] for ref in (left_ref, lo_ref, hi_ref, right_ref)], axis=0
        ).astype(jnp.float32)
        depth = None
        for turn in range(8):
            moved = pltpu.roll(window, 2 * count - turn, 0) if turn else window
            for j in range(taps):
                start = half - reach + j
                if start % 8 == turn:
                    term = moved[start - turn : start - turn + count] * taps_ref[j : j + 1, cols]
                    depth = term if depth is None else depth + term
        act_ref[:, cols] = (depth * jax.nn.sigmoid(depth)).astype(jnp.bfloat16)
    acts, points = [], []
    for (ref, copy), index in zip(views, blocks_of(quarters, cores, near)):
        if copy is not None:
            copy.wait()
        acts.append(act_ref[:, pl.ds(pl.multiple_of(index * channels, channels), channels)])
        points.append(
            jnp.concatenate(
                [ref[b * channels : (b + 1) * channels, :] for b in range(blocks)],
                axis=1,
            )
        )
    total = res_ref[...] + mm(jnp.concatenate(acts, axis=1), jnp.concatenate(points, axis=0))
    out_ref[...] = total.astype(jnp.bfloat16)


def shards(
    frames,
    expert_ids,
    gate_values,
    w_gate,
    w_up,
    w_down,
    norm_gain,
    norm_bias,
    point_in,
    depth_kernel,
    point_out,
):
    count, width = frames.shape
    wide = lax.axis_size("x") * lax.axis_size("z")
    quarters, cores = lax.axis_size("y"), lax.axis_size("c")
    narrow = quarters * cores
    experts = w_gate.shape[0] * wide
    slots = 2 * expert_ids.shape[1] * count // experts // cores
    share = width // quarters
    own = count // narrow
    taps, channels = depth_kernel.shape
    params = pltpu.CompilerParams(vmem_limit_bytes=VMEM_BYTES)

    in_hbm = lambda n: [pl.BlockSpec(memory_space=pltpu.HBM)] * n
    far = lambda array: pltpu.with_memory_space_constraint(array, pltpu.HBM)
    frames = far(frames)

    rows = experts * slots
    packed_rows = 3 * width + taps + 1
    outgoing, table, packed = pl.pallas_call(
        lambda *refs: prepare_kernel(experts, slots, *refs),
        in_specs=in_hbm(6),
        out_specs=in_vmem(3),
        out_shape=[
            jax.ShapeDtypeStruct((rows, share), jnp.bfloat16),
            jax.ShapeDtypeStruct((8, count), jnp.float32),
            jax.ShapeDtypeStruct((packed_rows, channels), jnp.bfloat16),
        ],
        scratch_shapes=[
            pltpu.VMEM((count, share), jnp.bfloat16),
            pltpu.VMEM((2, count), jnp.int32),
            pltpu.VMEM((2, count), jnp.float32),
            pltpu.VMEM((2 * width, channels), jnp.bfloat16),
            pltpu.VMEM((taps, channels), jnp.bfloat16),
            pltpu.VMEM((2 * width, channels), jnp.float32),
            pltpu.SemaphoreType.DMA((5 + narrow,)),
        ],
        compiler_params=params,
        name="prepare",
    )(
        far(expert_ids.T),
        frames,
        far(point_in.reshape(2 * width, channels)),
        far(depth_kernel),
        far(point_out),
        far(gate_values.T),
    )

    ring = [
        (y * cores + c, (y - 1 + 2 * c) % quarters * cores + c)
        for y in range(quarters)
        for c in range(cores)
    ]
    swap = [(i, cores - 1 - i) for i in range(cores)]
    around = lambda cells: lax.ppermute(cells, NARROW, ring)
    across = lambda cells: lax.ppermute(cells, "c", swap)
    held = [packed, around(packed)]

    def over(axis, cells):
        return lax.all_to_all(cells, axis, split_axis=0, concat_axis=0, tiled=True)

    arrived = over(WIDE, outgoing.reshape(experts, slots, share)).reshape(1, rows, share)
    mine = [w_gate[0], w_up[0], w_down[0]]
    theirs = [across(w) for w in mine]
    arrived, *held = lax.optimization_barrier((arrived, *held))
    swapped = [across(cells) for cells in held]
    held.append(around(held[-1]))
    repeated = pl.pallas_call(
        repeat_kernel,
        in_specs=in_vmem(1),
        out_specs=pl.BlockSpec(memory_space=pltpu.HBM),
        out_shape=jax.ShapeDtypeStruct((quarters, rows, share), jnp.bfloat16),
        scratch_shapes=[pltpu.SemaphoreType.DMA((quarters,))],
        compiler_params=params,
        name="repeat",
    )(arrived.reshape(rows, share))
    x = over("y", repeated)
    weights = mine + theirs
    partial = pl.pallas_call(
        expert_kernel,
        in_specs=in_vmem(1) + in_hbm(6),
        out_specs=pl.BlockSpec(memory_space=pltpu.VMEM),
        out_shape=jax.ShapeDtypeStruct((quarters, rows, share), jnp.bfloat16),
        scratch_shapes=[pltpu.VMEM(w.shape, w.dtype) for w in weights]
        + [pltpu.SemaphoreType.DMA((6,))],
        compiler_params=params,
        name="experts",
    )(x, *[far(w) for w in weights])
    partial = over("y", partial)
    summed = pl.pallas_call(
        sum_kernel,
        in_specs=in_vmem(1),
        out_specs=pl.BlockSpec(memory_space=pltpu.VMEM),
        out_shape=jax.ShapeDtypeStruct((rows, share), jnp.bfloat16),
        compiler_params=params,
        name="sum_parts",
    )(partial)
    summed, *held = lax.optimization_barrier((summed, *held, *swapped))
    held, swapped = held[: quarters - 1], held[quarters - 1 :]
    swapped.append(across(held[-1]))
    back = [(b, a) for a, b in ring]
    held.append(lax.ppermute(held[0], NARROW, back))
    swapped.append(lax.ppermute(held[0], NARROW, [(a, b ^ 1) for a, b in back]))
    returned = over(WIDE, summed.reshape(experts, slots, share)).reshape(rows, share)
    mixed = pl.pallas_call(
        combine_kernel,
        in_specs=in_vmem(2),
        out_specs=pl.BlockSpec(memory_space=pltpu.VMEM),
        out_shape=jax.ShapeDtypeStruct((count, share), jnp.bfloat16),
        compiler_params=params,
        name="combine",
    )(table, returned)
    held = held + swapped
    near = (0, 1, 2)
    held = [held[i] if i in near else far(held[i]) for i in order_of(narrow, near)]
    parts = over(NARROW, mixed.reshape(narrow, own, share))

    half = own // 2
    residual, lo, hi, kernel = pl.pallas_call(
        lambda *refs: norm_kernel(quarters, cores, near, *refs),
        in_specs=in_hbm(1) + in_vmem(3) + in_hbm(5) + in_vmem(3),
        out_specs=in_vmem(4),
        out_shape=[
            jax.ShapeDtypeStruct((own, width), jnp.float32),
            jax.ShapeDtypeStruct((half, width), jnp.bfloat16),
            jax.ShapeDtypeStruct((half, width), jnp.bfloat16),
            jax.ShapeDtypeStruct((taps + 1, width), jnp.float32),
        ],
        scratch_shapes=[
            pltpu.VMEM((own, width), jnp.bfloat16),
            pltpu.VMEM((narrow - 3, packed_rows - width, channels), jnp.bfloat16),
            pltpu.SemaphoreType.DMA((narrow + 1,)),
        ],
        compiler_params=params,
        name="norm_glu",
    )(frames, *held, parts, norm_gain[None, :], norm_bias[None, :])

    ends = wide * narrow - 1
    left = lax.ppermute(hi, EVERY, [(i, i + 1) for i in range(ends)])
    right = lax.ppermute(lo, EVERY, [(i + 1, i) for i in range(ends)])
    return pl.pallas_call(
        lambda *refs: conv_kernel(quarters, cores, near, taps, *refs),
        in_specs=in_vmem(3) + in_hbm(5) + in_vmem(6),
        out_specs=pl.BlockSpec(memory_space=pltpu.VMEM),
        out_shape=jax.ShapeDtypeStruct((own, width), jnp.bfloat16),
        scratch_shapes=[
            pltpu.VMEM((own, width), jnp.bfloat16),
            pltpu.VMEM((narrow - 3, width, channels), jnp.bfloat16),
            pltpu.SemaphoreType.DMA((narrow,)),
        ],
        compiler_params=params,
        name="conv",
    )(*held, left, lo, hi, right, kernel, residual)


def solution(mesh):
    chips = Mesh(mesh.devices.reshape(4, 16, 4, 2), EVERY)
    return jax.shard_map(
        shards,
        mesh=chips,
        in_specs=(
            P(WIDE, None),
            P(WIDE, None),
            P(WIDE, None),
            P(WIDE, None, NARROW),
            P(WIDE, None, NARROW),
            P(WIDE, NARROW, None),
            P(),
            P(),
            P(None, None, NARROW),
            P(None, NARROW),
            P(NARROW, None),
        ),
        out_specs=P(EVERY, None),
        check_vma=False,
    )
```

```python
import jax
import jax.numpy as jnp
from jax import lax
from jax.experimental import pallas as pl
from jax.experimental.pallas import tpu as pltpu
from jax.sharding import Mesh
from jax.sharding import PartitionSpec as P

WIDE = ("x", "z")
NARROW = ("y", "c")
EVERY = ("x", "z", "y", "c")
VMEM_BYTES = 24 << 20


def in_vmem(count):
    return [pl.BlockSpec(memory_space=pltpu.VMEM)] * count


def mm(a, b):
    return jnp.dot(a, b, preferred_element_type=jnp.float32)


def fetched(copies):
    for copy in copies:
        copy.start()
    return copies


def prepare_kernel(
    experts,
    slots,
    ids_ref,
    frames_ref,
    in_ref,
    taps_ref,
    point_ref,
    gates_ref,
    out_ref,
    table_ref,
    packed_ref,
    held_ref,
    ids_vmem,
    gates_vmem,
    in_vmem_ref,
    taps_vmem,
    wide_ref,
    sem,
):
    both, lanes = in_ref.shape
    half = both // 2
    taps = taps_ref.shape[0]
    at = both + taps + 1
    count, share = held_ref.shape
    column = pl.multiple_of(lax.axis_index("y") * share, share)
    names, held, halves, kernel, gates, *points = fetched(
        [
            pltpu.make_async_copy(ids_ref, ids_vmem, sem.at[0]),
            pltpu.make_async_copy(frames_ref.at[:, pl.ds(column, share)], held_ref, sem.at[1]),
            pltpu.make_async_copy(in_ref, in_vmem_ref, sem.at[2]),
            pltpu.make_async_copy(taps_ref, taps_vmem, sem.at[3]),
            pltpu.make_async_copy(gates_ref, gates_vmem, sem.at[4]),
        ]
        + [
            pltpu.make_async_copy(
                point_ref.at[:, b * lanes : (b + 1) * lanes],
                packed_ref.at[at + b * lanes : at + (b + 1) * lanes, :],
                sem.at[5 + b],
            )
            for b in range(point_ref.shape[1] // lanes)
        ]
    )
    names.wait()
    ids = ids_vmem[...]
    first = lax.axis_index("c") * slots
    expert = lax.broadcasted_iota(jnp.int32, (experts, count), 0)
    named = [jnp.where(expert == ids[k : k + 1, :], 1.0, 0.0) for k in range(2)]
    before = lax.broadcasted_iota(jnp.int32, (count, count), 0) < lax.broadcasted_iota(
        jnp.int32, (count, count), 1
    )
    rank = mm(
        jnp.concatenate(named, axis=0).astype(jnp.bfloat16),
        jnp.where(before, 1.0, 0.0).astype(jnp.bfloat16),
    )
    total = jnp.sum(named[0], axis=1, keepdims=True)
    place = [
        jnp.sum(named[0] * rank[:experts], axis=0, keepdims=True),
        jnp.sum(named[1] * (rank[experts:] + total), axis=0, keepdims=True),
    ]
    row = lax.broadcasted_iota(jnp.int32, (experts * slots, count), 0)
    chosen = None
    targets = []
    for k in range(2):
        local = place[k].astype(jnp.int32) - first
        target = jnp.where(
            (local >= 0) & (local < slots), ids[k : k + 1, :] * slots + local, -1
        )
        targets.append(target.astype(jnp.float32))
        hit = row == target
        chosen = hit if chosen is None else chosen | hit
    pick = jnp.where(chosen, 1.0, 0.0).astype(jnp.bfloat16)
    held.wait()
    out_ref[...] = mm(pick, held_ref[...]).astype(jnp.bfloat16)
    halves.wait()
    wide_ref[...] = in_vmem_ref[...].astype(jnp.float32)
    packed_ref[:half, :] = wide_ref[pl.ds(0, half, 2), :].astype(jnp.bfloat16)
    packed_ref[half:both, :] = wide_ref[pl.ds(1, half, 2), :].astype(jnp.bfloat16)
    kernel.wait()
    packed_ref[both:at, :] = jnp.concatenate(
        [taps_vmem[...].astype(jnp.float32), jnp.zeros((1, lanes), jnp.float32)], axis=0
    ).astype(jnp.bfloat16)
    gates.wait()
    table_ref[...] = jnp.concatenate(
        targets + [gates_vmem[...], jnp.zeros((4, count), jnp.float32)], axis=0
    )
    for copy in points:
        copy.wait()


def repeat_kernel(cells_ref, out_ref, sem):
    for copy in fetched(
        [
            pltpu.make_async_copy(cells_ref, out_ref.at[q], sem.at[q])
            for q in range(out_ref.shape[0])
        ]
    ):
        copy.wait()


def sum_kernel(parts_ref, out_ref):
    total = parts_ref[0].astype(jnp.float32)
    for q in range(1, parts_ref.shape[0]):
        total = total + parts_ref[q].astype(jnp.float32)
    out_ref[...] = total.astype(jnp.bfloat16)


def expert_kernel(x_ref, *refs):
    sources, out_ref, held, sem = refs[:6], refs[6], refs[7:13], refs[13]
    copies = [pltpu.make_async_copy(s, h, sem.at[i]) for i, (s, h) in enumerate(zip(sources, held))]
    for i in (0, 1, 3, 4, 2, 5):
        copies[i].start()
    chunks, _, width = x_ref.shape
    x = jnp.concatenate([x_ref[q] for q in range(chunks)], axis=1)
    hidden = []
    for pair in range(2):
        copies[3 * pair].wait()
        gate = mm(x, held[3 * pair][...])
        copies[3 * pair + 1].wait()
        up = mm(x, held[3 * pair + 1][...])
        hidden.append((gate * jax.nn.sigmoid(gate) * up).astype(jnp.bfloat16))
    copies[2].wait()
    copies[5].wait()
    for q in range(chunks):
        cols = slice(q * width, (q + 1) * width)
        out_ref[q] = (mm(hidden[0], held[2][:, cols]) + mm(hidden[1], held[5][:, cols])).astype(
            jnp.bfloat16
        )


def blocks_of(quarters, cores, near):
    y, c = lax.axis_index("y"), lax.axis_index("c")
    index = [
        lax.rem(y + (1 - 2 * side) * step + quarters, quarters) * cores + side
        for side in (c, cores - 1 - c)
        for step in range(quarters)
    ]
    return [index[i] for i in order_of(len(index), near)]


def order_of(count, near):
    return [i for i in range(count) if i in near] + [i for i in range(count)[::-1] if i not in near]


def fetched_rows(near, first, last, refs, held_ref, sem):
    views = [(ref.at[first:last, :], None) for ref in refs[: len(near)]]
    for i, ref in enumerate(refs[len(near) :]):
        copy = pltpu.make_async_copy(ref.at[first:last, :], held_ref.at[i], sem.at[i])
        copy.start()
        views.append((held_ref.at[i], copy))
    return views


def combine_kernel(table_ref, rows_ref, out_ref):
    count = table_ref.shape[1]
    table = table_ref[...].T
    slot = lax.broadcasted_iota(jnp.int32, (count, rows_ref.shape[0]), 1)
    hits = [
        jnp.where(slot == table[:, k : k + 1].astype(jnp.int32), 1.0, 0.0).astype(jnp.bfloat16)
        for k in range(2)
    ]
    picked = mm(jnp.concatenate(hits, axis=0), rows_ref[...])
    total = picked[:count] * table[:, 2:3] + picked[count:] * table[:, 3:4]
    out_ref[...] = total.astype(jnp.bfloat16)


def norm_kernel(quarters, cores, near, frames_ref, *refs):
    count = quarters * cores
    parts_ref, gain_ref, bias_ref, res_ref, lo_ref, hi_ref, taps_ref, own_ref, held_ref, sem = refs[count:]
    own, width = own_ref.shape
    index = lax.axis_index("y") * cores + lax.axis_index("c")
    fetch = pltpu.make_async_copy(
        frames_ref.at[pl.ds(pl.multiple_of(index * own, own), own), :], own_ref, sem.at[count]
    )
    fetch.start()
    views = fetched_rows(near, 0, held_ref.shape[1], refs[:count], held_ref, sem)
    moe = jnp.concatenate(
        [
            parts_ref[2 * q].astype(jnp.float32) + parts_ref[2 * q + 1].astype(jnp.float32)
            for q in range(parts_ref.shape[0] // 2)
        ],
        axis=1,
    )
    fetch.wait()
    residual = own_ref[...].astype(jnp.float32) + moe
    res_ref[...] = residual
    centered = residual - jnp.mean(residual, axis=1, keepdims=True)
    variance = jnp.mean(centered * centered, axis=1, keepdims=True)
    normed = (centered / jnp.sqrt(variance + 1e-05) * gain_ref[...] + bias_ref[...]).astype(
        jnp.bfloat16
    )
    channels = width // count
    half, taps = lo_ref.shape[0], taps_ref.shape[0]
    for (ref, copy), index in zip(views, blocks_of(quarters, cores, near)):
        if copy is not None:
            copy.wait()
        both = jnp.concatenate([ref[:width, :], ref[width : 2 * width, :]], axis=1)
        projected = mm(normed, both)
        glu = projected[:, :channels] * jax.nn.sigmoid(projected[:, channels:])
        glu = glu.astype(jnp.bfloat16)
        cols = pl.ds(pl.multiple_of(index * channels, channels), channels)
        lo_ref[:, cols] = glu[:half]
        hi_ref[:, cols] = glu[half:]
        taps_ref[:, cols] = ref[2 * width : 2 * width + taps, :].astype(jnp.float32)


def conv_kernel(quarters, cores, near, taps, *refs):
    blocks = quarters * cores
    left_ref, lo_ref, hi_ref, right_ref, taps_ref, res_ref, out_ref, act_ref, held_ref, sem = refs[blocks:]
    half, width = lo_ref.shape
    count = 2 * half
    reach = (taps - 1) // 2
    channels = width // blocks
    first = 2 * width + taps + 1
    views = fetched_rows(near, first, first + width, refs[:blocks], held_ref, sem)
    for n in range(0, blocks, 2):
        cols = slice(n * channels, (n + 2) * channels)
        window = jnp.concatenate(
            [ref[:, cols] for ref in (left_ref, lo_ref, hi_ref, right_ref)], axis=0
        ).astype(jnp.float32)
        depth = None
        for turn in range(8):
            moved = pltpu.roll(window, 2 * count - turn, 0) if turn else window
            for j in range(taps):
                start = half - reach + j
                if start % 8 == turn:
                    term = moved[start - turn : start - turn + count] * taps_ref[j : j + 1, cols]
                    depth = term if depth is None else depth + term
        act_ref[:, cols] = (depth * jax.nn.sigmoid(depth)).astype(jnp.bfloat16)
    acts, points = [], []
    for (ref, copy), index in zip(views, blocks_of(quarters, cores, near)):
        if copy is not None:
            copy.wait()
        acts.append(act_ref[:, pl.ds(pl.multiple_of(index * channels, channels), channels)])
        points.append(
            jnp.concatenate(
                [ref[b * channels : (b + 1) * channels, :] for b in range(blocks)],
                axis=1,
            )
        )
    total = res_ref[...] + mm(jnp.concatenate(acts, axis=1), jnp.concatenate(points, axis=0))
    out_ref[...] = total.astype(jnp.bfloat16)


def shards(
    frames,
    expert_ids,
    gate_values,
    w_gate,
    w_up,
    w_down,
    norm_gain,
    norm_bias,
    point_in,
    depth_kernel,
    point_out,
):
    count, width = frames.shape
    wide = lax.axis_size("x") * lax.axis_size("z")
    quarters, cores = lax.axis_size("y"), lax.axis_size("c")
    narrow = quarters * cores
    experts = w_gate.shape[0] * wide
    slots = 2 * expert_ids.shape[1] * count // experts // cores
    share = width // quarters
    own = count // narrow
    taps, channels = depth_kernel.shape
    params = pltpu.CompilerParams(vmem_limit_bytes=VMEM_BYTES)

    in_hbm = lambda n: [pl.BlockSpec(memory_space=pltpu.HBM)] * n
    far = lambda array: pltpu.with_memory_space_constraint(array, pltpu.HBM)
    frames = far(frames)

    rows = experts * slots
    packed_rows = 3 * width + taps + 1
    outgoing, table, packed = pl.pallas_call(
        lambda *refs: prepare_kernel(experts, slots, *refs),
        in_specs=in_hbm(6),
        out_specs=in_vmem(3),
        out_shape=[
            jax.ShapeDtypeStruct((rows, share), jnp.bfloat16),
            jax.ShapeDtypeStruct((8, count), jnp.float32),
            jax.ShapeDtypeStruct((packed_rows, channels), jnp.bfloat16),
        ],
        scratch_shapes=[
            pltpu.VMEM((count, share), jnp.bfloat16),
            pltpu.VMEM((2, count), jnp.int32),
            pltpu.VMEM((2, count), jnp.float32),
            pltpu.VMEM((2 * width, channels), jnp.bfloat16),
            pltpu.VMEM((taps, channels), jnp.bfloat16),
            pltpu.VMEM((2 * width, channels), jnp.float32),
            pltpu.SemaphoreType.DMA((5 + narrow,)),
        ],
        compiler_params=params,
        name="prepare",
    )(
        far(expert_ids.T),
        frames,
        far(point_in.reshape(2 * width, channels)),
        far(depth_kernel),
        far(point_out),
        far(gate_values.T),
    )

    ring = [
        (y * cores + c, (y - 1 + 2 * c) % quarters * cores + c)
        for y in range(quarters)
        for c in range(cores)
    ]
    swap = [(i, cores - 1 - i) for i in range(cores)]
    around = lambda cells: lax.ppermute(cells, NARROW, ring)
    across = lambda cells: lax.ppermute(cells, "c", swap)
    held = [packed, around(packed)]

    def over(axis, cells):
        return lax.all_to_all(cells, axis, split_axis=0, concat_axis=0, tiled=True)

    arrived = over(WIDE, outgoing.reshape(experts, slots, share)).reshape(1, rows, share)
    mine = [w_gate[0], w_up[0], w_down[0]]
    theirs = [across(w) for w in mine]
    arrived, *held = lax.optimization_barrier((arrived, *held))
    swapped = [across(cells) for cells in held]
    held.append(around(held[-1]))
    repeated = pl.pallas_call(
        repeat_kernel,
        in_specs=in_vmem(1),
        out_specs=pl.BlockSpec(memory_space=pltpu.HBM),
        out_shape=jax.ShapeDtypeStruct((quarters, rows, share), jnp.bfloat16),
        scratch_shapes=[pltpu.SemaphoreType.DMA((quarters,))],
        compiler_params=params,
        name="repeat",
    )(arrived.reshape(rows, share))
    x = over("y", repeated)
    weights = mine + theirs
    partial = pl.pallas_call(
        expert_kernel,
        in_specs=in_vmem(1) + in_hbm(6),
        out_specs=pl.BlockSpec(memory_space=pltpu.VMEM),
        out_shape=jax.ShapeDtypeStruct((quarters, rows, share), jnp.bfloat16),
        scratch_shapes=[pltpu.VMEM(w.shape, w.dtype) for w in weights]
        + [pltpu.SemaphoreType.DMA((6,))],
        compiler_params=params,
        name="experts",
    )(x, *[far(w) for w in weights])
    partial = over("y", partial)
    summed = pl.pallas_call(
        sum_kernel,
        in_specs=in_vmem(1),
        out_specs=pl.BlockSpec(memory_space=pltpu.VMEM),
        out_shape=jax.ShapeDtypeStruct((rows, share), jnp.bfloat16),
        compiler_params=params,
        name="sum_parts",
    )(partial)
    summed, *held = lax.optimization_barrier((summed, *held, *swapped))
    held, swapped = held[: quarters - 1], held[quarters - 1 :]
    swapped.append(across(held[-1]))
    back = [(b, a) for a, b in ring]
    held.append(lax.ppermute(held[0], NARROW, back))
    swapped.append(lax.ppermute(held[0], NARROW, [(a, b ^ 1) for a, b in back]))
    returned = over(WIDE, summed.reshape(experts, slots, share)).reshape(rows, share)
    mixed = pl.pallas_call(
        combine_kernel,
        in_specs=in_vmem(2),
        out_specs=pl.BlockSpec(memory_space=pltpu.VMEM),
        out_shape=jax.ShapeDtypeStruct((count, share), jnp.bfloat16),
        compiler_params=params,
        name="combine",
    )(table, returned)
    held = held + swapped
    near = (0, 1, 2)
    held = [held[i] if i in near else far(held[i]) for i in order_of(narrow, near)]
    parts = over(NARROW, mixed.reshape(narrow, own, share))

    half = own // 2
    residual, lo, hi, kernel = pl.pallas_call(
        lambda *refs: norm_kernel(quarters, cores, near, *refs),
        in_specs=in_hbm(1) + in_vmem(3) + in_hbm(5) + in_vmem(3),
        out_specs=in_vmem(4),
        out_shape=[
            jax.ShapeDtypeStruct((own, width), jnp.float32),
            jax.ShapeDtypeStruct((half, width), jnp.bfloat16),
            jax.ShapeDtypeStruct((half, width), jnp.bfloat16),
            jax.ShapeDtypeStruct((taps + 1, width), jnp.float32),
        ],
        scratch_shapes=[
            pltpu.VMEM((own, width), jnp.bfloat16),
            pltpu.VMEM((narrow - 3, packed_rows - width, channels), jnp.bfloat16),
            pltpu.SemaphoreType.DMA((narrow + 1,)),
        ],
        compiler_params=params,
        name="norm_glu",
    )(frames, *held, parts, norm_gain[None, :], norm_bias[None, :])

    ends = wide * narrow - 1
    left = lax.ppermute(hi, EVERY, [(i, i + 1) for i in range(ends)])
    right = lax.ppermute(lo, EVERY, [(i + 1, i) for i in range(ends)])
    return pl.pallas_call(
        lambda *refs: conv_kernel(quarters, cores, near, taps, *refs),
        in_specs=in_vmem(3) + in_hbm(5) + in_vmem(6),
        out_specs=pl.BlockSpec(memory_space=pltpu.VMEM),
        out_shape=jax.ShapeDtypeStruct((own, width), jnp.bfloat16),
        scratch_shapes=[
            pltpu.VMEM((own, width), jnp.bfloat16),
            pltpu.VMEM((narrow - 3, width, channels), jnp.bfloat16),
            pltpu.SemaphoreType.DMA((narrow,)),
        ],
        compiler_params=params,
        name="conv",
    )(*held, left, lo, hi, right, kernel, residual)


def solution(mesh):
    chips = Mesh(mesh.devices.reshape(4, 16, 4, 2), EVERY)
    return jax.shard_map(
        shards,
        mesh=chips,
        in_specs=(
            P(WIDE, None),
            P(WIDE, None),
            P(WIDE, None),
            P(WIDE, None, NARROW),
            P(WIDE, None, NARROW),
            P(WIDE, NARROW, None),
            P(),
            P(),
            P(None, None, NARROW),
            P(None, NARROW),
            P(NARROW, None),
        ),
        out_specs=P(EVERY, None),
        check_vma=False,
    )
```
